32 devices in a mesh: grp: 4 (over y, x), blk: 8 (over z, core).
Axes of the slice: x: 2, y: 2, z: 4, core: 2. Of those that a mesh axis runs over, the one named last changes fastest.
Arguments:
- estimate: float32 [32, 256, 256], P('blk'), may hold values from 0.25 to 4
- measured: bfloat16 [6, 256, 32, 256], P(None, 'blk'), may hold values from 0.25 to 4
- tile_plane: int32 [6, 256], P(None, 'blk'), may hold values from 0 to 31, as said below
- tile_strip: int32 [6, 256], P(None, 'blk'), may hold values from 0 to 7, as said below
- view_group: int32 [6], replicated, may hold values from 0 to 3, as said below
- kernel_cols: float32 [6, 3, 31], replicated, may hold values from 0.002 to 0.1
- kernel_rows: float32 [6, 3, 31], replicated, may hold values from 0.002 to 0.1
- kernel_planes: float32 [6, 3, 31], replicated, may hold values from 0.002 to 0.1
Outputs:
- updated: float32 [32, 256, 256], P('blk')
The draws below stay inside these ranges and needn't reach their ends.
Inputs may be any that keep to these rules, and one draw needn't show every extreme that they name: For each view the pairs (tile_plane, tile_strip) name every plane and strip exactly once; the 32 tiles of one view on one device of blk hold exactly 4 tiles of every block of 4 consecutive planes and exactly 4 tiles of every strip. `tile_strip`: see tile_plane. `view_group`: every group has at least one view and at most 2; some group has exactly 2.
All inputs are finite; a program needn't handle non-finite values.
Results may differ from the reference program's by a relative error of at most 0.0003.
Values may be sent and summed in bfloat16 or wider, within the bound.
A program may use at most 128 MiB of HBM per device.

```python
import math
import jax
import jax.numpy as jnp
from jax import lax

NX = 256
NY = 256
CZ = 4
VIEWS = 6
RANK = 3
TAPS = 31
NZ = 32
PY = 32
TILES = 256
N_GRP = 4
N_BLK = 8


def tile_layout(key):
    holders = N_BLK
    listing = []
    for view in range(VIEWS):
        view_key = jax.random.fold_in(key, view)
        sigma = jax.random.permutation(jax.random.fold_in(view_key, 1), holders)
        shuffle = jax.random.permutation(jax.random.fold_in(view_key, 2), holders)
        inverse = jnp.zeros((holders,), jnp.int32).at[shuffle].set(jnp.arange(holders, dtype=jnp.int32))
        holder = jnp.arange(holders, dtype=jnp.int32)[:, None]
        owner = jnp.arange(holders, dtype=jnp.int32)[None, :]
        strip = inverse[(holder - sigma[owner]) % holders]
        plane = owner[:, :, None] * CZ + jnp.arange(CZ, dtype=jnp.int32)[None, None, :]
        ident = (plane * holders + strip[:, :, None]).reshape(holders, holders * CZ)
        ident = jax.random.permutation(jax.random.fold_in(view_key, 3), ident, axis=1, independent=True)
        listing.append(ident.reshape(-1))
    return jnp.stack(listing).astype(jnp.int32)


def draw_tile_plane(key, part):
    return (tile_layout(key) // N_BLK).astype(jnp.int32)


def draw_tile_strip(key, part):
    return (tile_layout(key) % N_BLK).astype(jnp.int32)


def draw_view_group(key, part):
    base = jnp.arange(VIEWS, dtype=jnp.int32) % N_GRP
    relabel = jax.random.permutation(jax.random.fold_in(key, 11), N_GRP).astype(jnp.int32)
    return jax.random.permutation(jax.random.fold_in(key, 12), relabel[base]).astype(jnp.int32)


def level_of(stream_key, shape, shards, low, largest):
    loudness, own = 1.0, jax.random.fold_in(stream_key, 6)
    for dim, shards_of in shards:
        draws = jnp.exp(jax.random.uniform(jax.random.fold_in(own, dim), (shards_of,), jnp.float32, low / len(shards), largest / len(shards)))
        loudness = loudness * jnp.repeat(draws, shape[dim] // shards_of).reshape([-1 if axis == dim else 1 for axis in range(len(shape))])
    return loudness


def setup_inputs(seed: int = 0) -> dict:
    streams_of = jax.random.split(jax.random.key(seed), 9)
    estimate = jnp.clip(jnp.exp(math.log(4.0) - 2.7725887 * jax.random.uniform(streams_of[0], (NZ, NY, NX), jnp.float32) ** level_of(streams_of[0], (NZ, NY, NX), ((0, 8),), -0.2, 0.2)), 0.25, 4.0)
    measured = jnp.clip(jnp.exp(math.log(4.0) - 2.7725887 * jax.random.uniform(streams_of[1], (VIEWS, TILES, PY, NX), jnp.float32) ** level_of(streams_of[1], (VIEWS, TILES, PY, NX), ((1, 8),), -0.2, 0.2)), 0.25, 4.0).astype(jnp.bfloat16)
    tile_plane = draw_tile_plane(jax.random.fold_in(streams_of[8], 71), 0)
    tile_strip = draw_tile_strip(jax.random.fold_in(streams_of[8], 71), 0)
    view_group = draw_view_group(jax.random.fold_in(streams_of[8], 71), 0)
    kernel_cols = jnp.clip(jnp.exp(jax.random.uniform(streams_of[5], (VIEWS, RANK, TAPS), jnp.float32, math.log(0.002), math.log(0.1))), 0.002, 0.1)
    kernel_rows = jnp.clip(jnp.exp(jax.random.uniform(streams_of[6], (VIEWS, RANK, TAPS), jnp.float32, math.log(0.002), math.log(0.1))), 0.002, 0.1)
    kernel_planes = jnp.clip(jnp.exp(jax.random.uniform(streams_of[7], (VIEWS, RANK, TAPS), jnp.float32, math.log(0.002), math.log(0.1))), 0.002, 0.1)
    return {"estimate": estimate, "measured": measured, "tile_plane": tile_plane, "tile_strip": tile_strip, "view_group": view_group, "kernel_cols": kernel_cols, "kernel_rows": kernel_rows, "kernel_planes": kernel_planes}


def banded(taps, length):
    width = taps.shape[-1]
    half = width // 2
    position = jnp.arange(length, dtype=jnp.int32)
    offsets = position[None, :] - position[:, None] + half
    onehot = (offsets[:, :, None] == jnp.arange(width, dtype=jnp.int32)[None, None, :]).astype(jnp.float32)
    return jnp.einsum("imt,rt->rim", onehot, taps, precision=lax.Precision.HIGHEST)


def reference(estimate, measured, tile_plane, tile_strip, view_group, kernel_cols, kernel_rows, kernel_planes):
    highest = lax.Precision.HIGHEST
    group_sums = jnp.zeros((N_GRP, NZ, NY, NX), jnp.float32)
    group_sizes = jnp.zeros((N_GRP,), jnp.float32)
    for view in range(VIEWS):
        positions = (tile_plane[view] * N_BLK + tile_strip[view]).astype(jnp.int32)
        observed = jnp.zeros((NZ * N_BLK, PY, NX), jnp.bfloat16).at[positions].set(measured[view]).reshape(NZ, NY, NX)
        band_cols = banded(kernel_cols[view], NX)
        band_rows = banded(kernel_rows[view], NY)
        band_planes = banded(kernel_planes[view], NZ)
        rank_terms = jnp.einsum("zym,rim->rzyi", estimate, band_cols, precision=highest)
        rank_terms = jnp.einsum("rzmx,rim->rzix", rank_terms, band_rows, precision=highest)
        blurred = jnp.einsum("rmyx,rim->iyx", rank_terms, band_planes, precision=highest)
        ratios = observed.astype(jnp.float32) / blurred
        adjoint = jnp.einsum("iyx,rim->rmyx", ratios, band_planes, precision=highest)
        adjoint = jnp.einsum("rzix,rim->rzmx", adjoint, band_rows, precision=highest)
        factor = jnp.einsum("rzyi,rim->zym", adjoint, band_cols, precision=highest)
        membership = (view_group[view] == jnp.arange(N_GRP, dtype=jnp.int32)).astype(jnp.float32)
        group_sums = group_sums + membership[:, None, None, None] * factor[None]
        group_sizes = group_sizes + membership
    log_mean = jnp.sum(jnp.log(group_sums / group_sizes[:, None, None, None]), axis=0)
    return estimate * jnp.exp(log_mean / N_GRP)
```

```python
import jax
import jax.numpy as jnp
from jax import lax
from jax.experimental import pallas as pl
from jax.experimental.pallas import tpu as pltpu
from jax.sharding import PartitionSpec as P

VSLOT = 2
HIGH = lax.Precision.HIGH


MESH = pl.DeviceIdType.MESH


def band_kernel(*refs):
    count = len(refs) // 2
    for row, out in zip(refs[:count], refs[count:]):
        number, rows, cols = out.shape
        for n in range(number):
            wide = jnp.broadcast_to(row[n], (rows, row.shape[-1]))
            wide = pltpu.roll(wide, 0, 1, stride=1, stride_axis=0)
            out[n] = wide[:, :cols]


def bands(shapes):
    rows_in, outs = [], []
    for taps, rows, cols, lead in shapes:
        number, width = taps.shape
        half = width // 2
        span = -(-(max(cols, rows) + lead + width) // 128) * 128
        row = jnp.pad(taps, ((0, 0), (0, span - width)))
        row = jnp.roll(row, lead - half, axis=1)
        rows_in.append(row[:, None, :])
        outs.append(jax.ShapeDtypeStruct((number, rows, cols), jnp.float32))
    vmem = pl.BlockSpec(memory_space=pltpu.VMEM)
    return pl.pallas_call(
        band_kernel,
        out_shape=outs,
        in_specs=[vmem] * len(outs),
        out_specs=[vmem] * len(outs),
    )(*rows_in)


def spread_kernel(blocks, groups, step, padded, planes, tiles, pencil, got, arrived, sa, ra, sb, rb, sp, rp, st, rt):
    me = lax.axis_index("blk")
    grp = lax.axis_index("grp")
    cz, span = pencil.shape[1], pencil.shape[2]
    cq = cz // groups
    mine = pl.ds(grp * cq, cq)
    barrier = pltpu.get_barrier_semaphore()
    for k in range(1, groups):
        pl.semaphore_signal(barrier, inc=1, device_id=(lax.rem(grp + k, groups), me), device_id_type=MESH)
    for rel in range(1, blocks):
        pl.semaphore_signal(barrier, inc=1, device_id=(grp, lax.rem(me + rel, blocks)), device_id_type=MESH)
    pl.semaphore_wait(barrier, groups + blocks - 2)

    first, small, second, large = {}, {}, {}, {}
    for rel in range(1, blocks):
        dest = lax.rem(me + rel, blocks)
        first[rel] = pltpu.make_async_remote_copy(
            src_ref=padded.at[mine, pl.ds(dest * step, span)],
            dst_ref=pencil.at[me, mine],
            send_sem=sa.at[rel],
            recv_sem=ra.at[rel],
            device_id=(grp, dest),
            device_id_type=MESH,
        )
        first[rel].start()
    for rel in range(1, blocks):
        dest = lax.rem(me + rel, blocks)
        small[rel] = pltpu.make_async_remote_copy(
            src_ref=planes.at[dest],
            dst_ref=got.at[me],
            send_sem=sp.at[rel],
            recv_sem=rp.at[rel],
            device_id=(grp, dest),
            device_id_type=MESH,
        )
        small[rel].start()
    for rel in range(1, blocks):
        dest = lax.rem(me + rel, blocks)
        large[rel] = pltpu.make_async_remote_copy(
            src_ref=tiles.at[dest],
            dst_ref=arrived.at[me],
            send_sem=st.at[rel],
            recv_sem=rt.at[rel],
            device_id=(grp, dest),
            device_id_type=MESH,
        )
        large[rel].start()
    arrived[me] = tiles[me]
    pencil[me] = padded[:, pl.ds(me * step, span)]
    got[me] = planes[me]
    for rel in range(1, blocks):
        src = lax.rem(me + blocks - rel, blocks)
        landed = pencil.at[src, mine]
        pltpu.make_async_remote_copy(
            src_ref=landed,
            dst_ref=landed,
            send_sem=sa.at[rel],
            recv_sem=ra.at[rel],
            device_id=(grp, src),
            device_id_type=MESH,
        ).wait_recv()
        for k in range(1, groups):
            second[rel, k] = pltpu.make_async_remote_copy(
                src_ref=landed,
                dst_ref=landed,
                send_sem=sb.at[rel, k - 1],
                recv_sem=rb.at[rel, k - 1],
                device_id=(lax.rem(grp + k, groups), me),
                device_id_type=MESH,
            )
            second[rel, k].start()
    for rel in range(1, blocks):
        src = lax.rem(me + blocks - rel, blocks)
        for k in range(1, groups):
            peer = lax.rem(grp + groups - k, groups)
            theirs = pencil.at[src, pl.ds(peer * cq, cq)]
            pltpu.make_async_remote_copy(
                src_ref=theirs,
                dst_ref=theirs,
                send_sem=sb.at[rel, k - 1],
                recv_sem=rb.at[rel, k - 1],
                device_id=(peer, me),
                device_id_type=MESH,
            ).wait_recv()
        pltpu.make_async_remote_copy(
            src_ref=planes.at[src],
            dst_ref=got.at[src],
            send_sem=sp.at[rel],
            recv_sem=rp.at[rel],
            device_id=(grp, src),
            device_id_type=MESH,
        ).wait_recv()
        pltpu.make_async_remote_copy(
            src_ref=tiles.at[src],
            dst_ref=arrived.at[src],
            send_sem=st.at[rel],
            recv_sem=rt.at[rel],
            device_id=(grp, src),
            device_id_type=MESH,
        ).wait_recv()
    for copies in (first, small, second, large):
        for copy in copies.values():
            copy.wait_send()


def spread(estimate, planes, tiles, lead, blocks, groups):
    cz, ny, nx = estimate.shape
    py = ny // blocks
    chunk = min(py, lead)
    span = (py + 2 * lead) // chunk
    padded = jnp.pad(estimate, ((0, 0), (lead, lead), (0, 0))).reshape(cz, -1, chunk, nx)
    vmem = pl.BlockSpec(memory_space=pltpu.VMEM)
    dma = pltpu.SemaphoreType.DMA
    pencil, got, arrived = pl.pallas_call(
        lambda *refs: spread_kernel(blocks, groups, py // chunk, *refs),
        out_shape=[
            jax.ShapeDtypeStruct((blocks, cz, span, chunk, nx), jnp.float32),
            jax.ShapeDtypeStruct(planes.shape, jnp.int32),
            jax.ShapeDtypeStruct(tiles.shape, tiles.dtype),
        ],
        in_specs=[vmem] * 3,
        out_specs=[vmem] * 3,
        scratch_shapes=[
            dma((blocks,)),
            dma((blocks,)),
            dma((blocks, groups - 1)),
            dma((blocks, groups - 1)),
            dma((blocks,)),
            dma((blocks,)),
            dma((blocks,)),
            dma((blocks,)),
        ],
        compiler_params=pltpu.CompilerParams(collective_id=1, has_side_effects=True),
        cost_estimate=pl.CostEstimate(flops=0, bytes_accessed=1 << 26, transcendentals=0),
        name="spread",
    )(padded, planes, tiles)
    return pencil.reshape(cz * blocks, py + 2 * lead, nx), got, arrived


def finish_kernel(blocks, groups, logs, est, out, got1, send2, got2, s1, r1, s2, r2, s3, r3):
    me = lax.axis_index("blk")
    grp = lax.axis_index("grp")
    cq = est.shape[0] // groups
    mine = pl.ds(grp * cq, cq)
    barrier = pltpu.get_barrier_semaphore()
    for k in range(1, groups):
        pl.semaphore_signal(barrier, inc=1, device_id=(lax.rem(grp + k, groups), me), device_id_type=MESH)
    for rel in range(1, blocks):
        pl.semaphore_signal(barrier, inc=1, device_id=(grp, lax.rem(me + rel, blocks)), device_id_type=MESH)
    pl.semaphore_wait(barrier, groups + blocks - 2)
    order = list(range(1, blocks)) + [0]

    first, second, third = {}, {}, {}
    for rel in order:
        dest = lax.rem(me + rel, blocks)
        for k in range(1, groups):
            peer = lax.rem(grp + k, groups)
            first[rel, k] = pltpu.make_async_remote_copy(
                src_ref=logs.at[dest, pl.ds(peer * cq, cq)],
                dst_ref=got1.at[rel, k - 1],
                send_sem=s1.at[rel, k - 1],
                recv_sem=r1.at[rel, k - 1],
                device_id=(peer, me),
                device_id_type=MESH,
            )
            first[rel, k].start()
    for rel in order:
        dest = lax.rem(me + rel, blocks)
        total = logs[dest, mine]
        for k in range(1, groups):
            first[rel, k].wait_recv()
            total = total + got1[rel, k - 1]
        if rel == 0:
            got2[0] = total
        else:
            send2[rel] = total
            second[rel] = pltpu.make_async_remote_copy(
                src_ref=send2.at[rel],
                dst_ref=got2.at[rel],
                send_sem=s2.at[rel],
                recv_sem=r2.at[rel],
                device_id=(grp, dest),
                device_id_type=MESH,
            )
            second[rel].start()
    for rel in order:
        strip = lax.rem(me + blocks - rel, blocks)
        if rel != 0:
            second[rel].wait_recv()
        out[mine, strip] = est[mine, strip] * jnp.exp(got2[rel] * (1.0 / groups))
        for k in range(1, groups):
            third[rel, k] = pltpu.make_async_remote_copy(
                src_ref=out.at[mine, strip],
                dst_ref=out.at[mine, strip],
                send_sem=s3.at[rel, k - 1],
                recv_sem=r3.at[rel, k - 1],
                device_id=(lax.rem(grp + k, groups), me),
                device_id_type=MESH,
            )
            third[rel, k].start()
    for copy in first.values():
        copy.wait_send()
    for copy in second.values():
        copy.wait_send()
    for copy in third.values():
        copy.wait_send()
    for rel in order:
        strip = lax.rem(me + blocks - rel, blocks)
        for k in range(1, groups):
            peer = lax.rem(grp + groups - k, groups)
            theirs = out.at[pl.ds(peer * cq, cq), strip]
            pltpu.make_async_remote_copy(
                src_ref=theirs,
                dst_ref=theirs,
                send_sem=s3.at[rel, k - 1],
                recv_sem=r3.at[rel, k - 1],
                device_id=(peer, me),
                device_id_type=MESH,
            ).wait_recv()


def finish(logs, estimate, blocks, groups):
    cz, ny, nx = estimate.shape
    py = ny // blocks
    cq = cz // groups
    vmem = pl.BlockSpec(memory_space=pltpu.VMEM)
    dma = pltpu.SemaphoreType.DMA
    out = pl.pallas_call(
        lambda *refs: finish_kernel(blocks, groups, *refs),
        out_shape=jax.ShapeDtypeStruct((cz, blocks, py, nx), jnp.float32),
        in_specs=[vmem, vmem],
        out_specs=vmem,
        scratch_shapes=[
            pltpu.VMEM((blocks, groups - 1, cq, py, nx), jnp.float32),
            pltpu.VMEM((blocks, cq, py, nx), jnp.float32),
            pltpu.VMEM((blocks, cq, py, nx), jnp.float32),
            dma((blocks, groups - 1)),
            dma((blocks, groups - 1)),
            dma((blocks,)),
            dma((blocks,)),
            dma((blocks, groups - 1)),
            dma((blocks, groups - 1)),
        ],
        compiler_params=pltpu.CompilerParams(collective_id=0, has_side_effects=True),
        name="finish",
    )(logs.reshape(blocks, cz, py, nx), estimate.reshape(cz, blocks, py, nx))
    return out.reshape(cz, ny, nx)


def general(estimate, measured, tile_plane, tile_strip, view_group, kernel_cols, kernel_rows, kernel_planes):
    cz, ny, nx = estimate.shape
    blocks = lax.axis_size("blk")
    groups = lax.axis_size("grp")
    nz = cz * blocks
    py = ny // blocks
    half = kernel_rows.shape[-1] // 2
    lead = -(-half // 8) * 8
    ext = py + 2 * lead
    tiles = measured.shape[1]
    per = tiles // blocks

    matches = (view_group == lax.axis_index("grp")).astype(jnp.int32)
    members = jnp.sum(matches).astype(jnp.float32)
    ids = jnp.arange(view_group.shape[0], dtype=jnp.int32)
    ranking = jnp.sum(jnp.where(ids[None, :] < ids[:, None], matches[None, :], 0), axis=1)
    picked = [matches * (ranking == s).astype(jnp.int32) for s in range(VSLOT)]
    chosen = [jnp.sum(p * ids) for p in picked]
    weights = jnp.stack([jnp.sum(p).astype(jnp.float32) / members for p in picked])

    pick = lambda a: jnp.stack([lax.dynamic_index_in_dim(a, c, 0, keepdims=False) for c in chosen])
    pieces, planes, strips = pick(measured), pick(tile_plane), pick(tile_strip)
    number = jnp.arange(tiles, dtype=jnp.int32)
    earlier = (strips[:, :, None] == strips[:, None, :]) & (number[None, :] < number[:, None])
    positions = strips * per + jnp.sum(earlier.astype(jnp.int32), axis=2)
    order = positions[:, None, :] == jnp.arange(tiles, dtype=jnp.int32)[None, :, None]
    send_planes = jnp.sum(jnp.where(order, planes[:, None, :], 0), axis=2)
    send = jnp.einsum("vpi,viyx->pvyx", order.astype(jnp.bfloat16), pieces)
    send = send.reshape(blocks, per, VSLOT, py, nx)

    table = send_planes.reshape(VSLOT, blocks, per).transpose(1, 0, 2)
    table = jnp.pad(table, ((0, 0), (0, 8 - VSLOT), (0, 128 - per)))
    pencil, table, got = spread(estimate, table, send, lead, blocks, groups)
    got = got.reshape(tiles, VSLOT, py, nx)
    got_planes = table[:, :VSLOT, :per].transpose(0, 2, 1).reshape(tiles, VSLOT)
    place = (got_planes[None] == jnp.arange(nz, dtype=jnp.int32)[:, None, None]).astype(jnp.bfloat16)
    observed = jnp.einsum("ptv,tvyx->vpyx", place, got).astype(jnp.float32)

    kc, kr, kp = pick(kernel_cols), pick(kernel_rows), pick(kernel_planes)
    flat = lambda k: k.reshape(-1, k.shape[-1])
    fold = lambda m: m.reshape((VSLOT, -1) + m.shape[1:])
    bx, by, bz = map(fold, bands([(flat(kc), nx, nx, 0), (flat(kr), py, ext, lead), (flat(kp), nz, nz, 0)]))
    byw = by * weights[:, None, None, None]

    t = jnp.einsum("zmx,vrim->vrzix", pencil, by, precision=HIGH)
    t = jnp.einsum("vrzix,vrnx->vrzin", t, bx, precision=HIGH)
    blurred = jnp.einsum("vrzin,vrpz->vpin", t, bz, precision=HIGH)
    ratios = observed / blurred
    a = jnp.einsum("vpin,vrpz->vrzin", ratios, bz, precision=HIGH)
    a = jnp.einsum("vrzin,vrnx->vrzix", a, bx, precision=HIGH)
    wide = jnp.einsum("vrzix,vrim->zmx", a, byw, precision=HIGH)

    chunk = min(py, lead)
    average = wide[:, lead : lead + py]
    for d in range(1, lead // chunk + 1):
        up = wide[:, lead + py + (d - 1) * chunk : lead + py + d * chunk]
        down = wide[:, lead - d * chunk : lead - (d - 1) * chunk]
        up = lax.ppermute(up, "blk", [(i, i + d) for i in range(blocks - d)])
        down = lax.ppermute(down, "blk", [(i, i - d) for i in range(d, blocks)])
        rest = py - chunk
        average = average + jnp.pad(up, ((0, 0), (0, rest), (0, 0))) + jnp.pad(down, ((0, 0), (rest, 0), (0, 0)))
    logs = jnp.log(average)
    return finish(logs, estimate, blocks, groups)


def prep_kernel(per, view_group, tile_plane, tile_strip, order, chosen, weights, table, count):
    views, tiles = tile_plane.shape
    grp = lax.axis_index("grp")
    total, first, second = jnp.int32(0), jnp.int32(0), jnp.int32(0)
    for view in range(views):
        match = view_group[view] == grp
        first = jnp.where(match & (total == 0), view, first)
        second = jnp.where(match & (total == 1), view, second)
        total = total + match.astype(jnp.int32)
    second = jnp.where(total < VSLOT, first, second)
    chosen[0] = first
    chosen[1] = second
    single = total < VSLOT
    weights[0] = jnp.where(single, 1.0, 1.0 / VSLOT)
    weights[1] = jnp.where(single, 0.0, 1.0 / VSLOT)
    for slot, view in enumerate((first, second)):
        for strip in range(tiles // per):
            count[strip] = 0
        for tile in range(tiles):
            strip = tile_strip[view, tile]
            seen = count[strip]
            count[strip] = seen + 1
            order[slot, strip * per + seen] = tile
            table[strip, pl.ds(slot * per + seen, 1), :] = jnp.full((1, 128), tile_plane[view, tile], jnp.int32)


def split(value):
    high = value.astype(jnp.bfloat16)
    low = (value - high.astype(jnp.float32)).astype(jnp.bfloat16)
    return high, low


def dot(a, b):
    return jnp.dot(a, b, preferred_element_type=jnp.float32)


def dot3(a, b):
    return dot(jnp.concatenate([a[0], a[1], a[0]], axis=1), jnp.concatenate([b[0], b[0], b[1]], axis=0))


EST = 16383.0
HALO = 65534.0
LOG = 32767.0
KNEE = 4.0


def to_code(value):
    return ((value + 0.5).astype(jnp.int32) - 32768).astype(jnp.int16)


def log_code(logs):
    return to_code(logs / (KNEE + jnp.abs(logs)) * LOG + 32768.0)


def log_of(code):
    value = code.astype(jnp.int32).astype(jnp.float32) * (1.0 / LOG)
    return KNEE * value / (1.0 - jnp.abs(value))


def halo_code(value):
    return to_code(value / (1.0 + value) * HALO)


def halo_of(code):
    value = (code.astype(jnp.int32) + 32768).astype(jnp.float32) * (1.0 / HALO)
    return value / (1.0 - value)


def fused_kernel(
    blocks, groups, lead,
    order, chosen, weights, table, est, measured, kc, kr, kp,
    lout,
    stage, ecode, pencil, sendt, arrived, got, rowbuf,
    bxt_h, bxt_l, bx_h, bx_l, kz_h, kz_l, kzt_h, kzt_l, byf, byt_h, byt_l, byw, pk,
    t1_h, t1_l, t2_h, t2_l, blur, obs, a2, own, up_s, dn_s, up_r, dn_r, logs_s, logs_r, mean_s,
    sm, sa, ra, sb, rb, sp, rp, st, rt, sh, rh, s1, r1, s2, r2, s3, r3,
):
    me = lax.axis_index("blk")
    grp = lax.axis_index("grp")
    cz, ny, nx = est.shape
    py = ny // blocks
    nz = cz * blocks
    ext = py + 2 * lead
    ranks, width = kc.shape[1], kc.shape[2]
    half = width // 2
    terms = VSLOT * ranks
    per = sendt.shape[1] // VSLOT
    tiles = per * blocks
    bands8 = py // 8
    wide = 8 * nz

    def remote(src, dst, send, recv, to):
        return pltpu.make_async_remote_copy(
            src_ref=src, dst_ref=dst, send_sem=send, recv_sem=recv, device_id=to, device_id_type=MESH
        )

    load = pltpu.make_async_copy(measured, stage, sm)
    load.start()
    barrier = pltpu.get_barrier_semaphore()
    for k in range(1, groups):
        pl.semaphore_signal(barrier, inc=1, device_id=(lax.rem(grp + k, groups), me), device_id_type=MESH)
    for rel in range(1, blocks):
        pl.semaphore_signal(barrier, inc=1, device_id=(grp, lax.rem(me + rel, blocks)), device_id_type=MESH)

    for c in range(cz):
        ecode[c, 0:lead, :] = jnp.full((lead, nx), -32768, jnp.int16)
        ecode[c, lead + ny : lead + ny + lead, :] = jnp.full((lead, nx), -32768, jnp.int16)
        ecode[c, lead : lead + ny, :] = to_code(est[c] * EST)
    pl.semaphore_wait(barrier, groups + blocks - 2)

    sends = []
    for rel in range(1, blocks):
        dest = lax.rem(me + rel, blocks)
        copy = remote(
            ecode.at[grp, pl.ds(pl.multiple_of(dest * py, py), ext)],
            pencil.at[me * cz + grp],
            sa.at[rel], ra.at[rel], (grp, dest),
        )
        copy.start()
        sends.append(copy)
    for rel in range(1, blocks):
        dest = lax.rem(me + rel, blocks)
        copy = remote(table.at[dest], got.at[me], sp.at[rel], rp.at[rel], (grp, dest))
        copy.start()
        sends.append(copy)
    load.wait()
    for rel in list(range(1, blocks)) + [0]:
        dest = lax.rem(me + rel, blocks)
        for slot in range(VSLOT):
            for j in range(per):
                sendt[dest, slot * per + j] = stage[chosen[slot], order[slot, dest * per + j]]
        if rel > 0:
            copy = remote(sendt.at[dest], arrived.at[me], st.at[rel], rt.at[rel], (grp, dest))
            copy.start()
            sends.append(copy)
    arrived[me] = sendt[me]
    got[me] = table[me]
    for c in range(cz):
        pencil[me * cz + c] = ecode[c, pl.ds(pl.multiple_of(me * py, py), ext), :]

    def row_of(taps, view):
        rowbuf[...] = jnp.zeros_like(rowbuf)
        rowbuf[0:ranks, 0:width] = taps[view]

    span = rowbuf.shape[1]
    for slot in range(VSLOT):
        view = chosen[slot]
        row_of(kc, view)
        for r in range(ranks):
            t = slot * ranks + r
            line = jnp.broadcast_to(rowbuf[r : r + 1, :], (nx, span))
            band = pltpu.roll(line, span - half, 1, stride=1, stride_axis=0)[:, :nx]
            bx_h[t], bx_l[t] = split(band)
            bxt_h[t], bxt_l[t] = split(band.T)
        row_of(kr, view)
        for r in range(ranks):
            t = slot * ranks + r
            line = jnp.broadcast_to(rowbuf[r : r + 1, 0:128], (py, 128))
            band = pltpu.roll(line, lead - half, 1, stride=1, stride_axis=0)
            byw[t * py : (t + 1) * py, :] = band * weights[slot]
            high, low = split(band[:, :ext] * (1.0 / EST))
            high, low = high.astype(jnp.float32), low.astype(jnp.float32)
            byf[t * py : (t + 1) * py, :] = jnp.concatenate([high * 256.0, high, low * 256.0], axis=1).astype(jnp.bfloat16)
        row_of(kp, view)
        spread8 = lax.broadcasted_iota(jnp.int32, (128, wide), 1) // 8
        spread8 = (spread8 == lax.broadcasted_iota(jnp.int32, (128, wide), 0)).astype(jnp.bfloat16)
        first = rowbuf[:, 0:128]
        p0, rest = split(first)
        p1, p2 = split(first - p0.astype(jnp.float32) )
        p2 = (first - p0.astype(jnp.float32) - p1.astype(jnp.float32)).astype(jnp.bfloat16)
        line8 = dot(p0, spread8) + dot(p1, spread8) + dot(p2, spread8)
        line8 = jnp.concatenate([line8, jnp.zeros_like(line8)], axis=1)
        for r in range(ranks):
            t = slot * ranks + r
            line = jnp.broadcast_to(line8[r : r + 1, :], (nz, 2 * wide))
            band = pltpu.roll(line, 2 * wide - 8 * half, 1, stride=8, stride_axis=0)[:, :wide]
            blur[t, 0:nz, :] = band
    turned = byw[...].T[0:ext, :]
    byt_h[0:ext, :], low = split(turned)
    byt_h[ext : 2 * ext, :] = low

    for rel in range(1, blocks):
        src = lax.rem(me + blocks - rel, blocks)
        remote(table.at[src], got.at[src], sp.at[rel], rp.at[rel], (grp, src)).wait_recv()
    for slot in range(VSLOT):
        for src in range(blocks):
            for j in range(per):
                tile = src * per + j
                pk[8 * tile : 8 * tile + 8, :] = jnp.broadcast_to(got[src, slot * per + j : slot * per + j + 1, :], (8, 128))
        lanes = lax.broadcasted_iota(jnp.int32, (wide, 128), 1)
        hot = (pk[...] == lanes).astype(jnp.float32).astype(jnp.bfloat16)[:, :nz]
        same = (lax.broadcasted_iota(jnp.int32, (wide, wide), 0) % 8) == (lax.broadcasted_iota(jnp.int32, (wide, wide), 1) % 8)
        for r in range(ranks):
            t = slot * ranks + r
            high, low = split(blur[t, 0:nz, :])
            high = jnp.where(same, dot(hot, high), 0.0)
            low = jnp.where(same, dot(hot, low), 0.0)
            kz_h[t] = high.astype(jnp.bfloat16)
            kz_l[t] = low.astype(jnp.bfloat16)
            kzt_h[t] = high.T.astype(jnp.bfloat16)
            kzt_l[t] = low.T.astype(jnp.bfloat16)

    for rel in range(1, blocks):
        src = lax.rem(me + blocks - rel, blocks)
        landed = pencil.at[src * cz + grp]
        remote(landed, landed, sa.at[rel], ra.at[rel], (grp, src)).wait_recv()
        for k in range(1, groups):
            copy = remote(landed, landed, sb.at[rel, k - 1], rb.at[rel, k - 1], (lax.rem(grp + k, groups), me))
            copy.start()
            sends.append(copy)

    def blur_rows(src):
        def step(i, carry):
            z = src * cz + 2 * i
            parts = []
            for d in range(2):
                code = pencil[z + d].astype(jnp.int32)
                high = ((code >> 8) + 128).astype(jnp.float32).astype(jnp.bfloat16)
                low = (code & 255).astype(jnp.float32).astype(jnp.bfloat16)
                parts.append(dot(byf[...], jnp.concatenate([high, low, high], axis=0)))
            place = pl.ds(pl.multiple_of(z * 8, 16), 16)
            for t in range(terms):
                for y in range(bands8):
                    at = t * py + 8 * y
                    both = jnp.concatenate([parts[0][at : at + 8], parts[1][at : at + 8]], axis=0)
                    high, low = split(both)
                    t1_h[t * bands8 + y, place, :] = high
                    t1_l[t * bands8 + y, place, :] = low
            return carry

        lax.fori_loop(0, cz // 2, step, 0)

    blur_rows(me)
    for rel in range(1, blocks):
        src = lax.rem(me + blocks - rel, blocks)
        for k in range(1, groups):
            peer = lax.rem(grp + groups - k, groups)
            theirs = pencil.at[src * cz + peer]
            remote(theirs, theirs, sb.at[rel, k - 1], rb.at[rel, k - 1], (peer, me)).wait_recv()
        blur_rows(src)

    def blur_cols(i, carry):
        t = i // bands8
        t2_h[i], t2_l[i] = split(dot3((t1_h[i], t1_l[i]), (bxt_h[t], bxt_l[t])))
        return carry

    lax.fori_loop(0, terms * bands8, blur_cols, 0)

    def blur_planes(i, carry):
        slot, y = i // bands8, i % bands8
        total = None
        for r in range(ranks):
            t = slot * ranks + r
            piece = dot3((kz_h[t], kz_l[t]), (t2_h[t * bands8 + y], t2_l[t * bands8 + y]))
            total = piece if total is None else total + piece
        blur[i] = total
        return carry

    lax.fori_loop(0, VSLOT * bands8, blur_planes, 0)

    for rel in range(blocks):
        src = lax.rem(me + blocks - rel, blocks)
        if rel > 0:
            remote(sendt.at[src], arrived.at[src], st.at[rel], rt.at[rel], (grp, src)).wait_recv()
        for slot in range(VSLOT):
            for j in range(per):
                tile = arrived[src, slot * per + j].astype(jnp.float32)
                for y in range(bands8):
                    obs[slot * bands8 + y, pl.ds(pl.multiple_of((src * per + j) * 8, 8), 8), :] = tile[8 * y : 8 * y + 8]

    def adjoint(i, carry):
        slot, y = i // bands8, i % bands8
        ratio = split(obs[i] / blur[i])
        for r in range(ranks):
            t = slot * ranks + r
            a1 = split(dot3((kzt_h[t], kzt_l[t]), ratio))
            a2[t * bands8 + y] = dot3(a1, (bx_h[t], bx_l[t]))
        return carry

    lax.fori_loop(0, VSLOT * bands8, adjoint, 0)

    def halo(rel, up):
        k = lax.rem(me + rel, blocks)
        rows = pl.ds(k * cz, cz)
        if up:
            return remote(up_s.at[rows], dn_r.at[rows], sh.at[k, 0], rh.at[k, 0], (grp, me - 1))
        return remote(dn_s.at[rows], up_r.at[rows], sh.at[k, 1], rh.at[k, 1], (grp, me + 1))

    for rel in range(1, blocks + 1):
        k = lax.rem(me + rel, blocks)

        def back(c, carry):
            z = k * cz + c
            at = pl.ds(pl.multiple_of(z * 8, 8), 8)
            column = jnp.concatenate([a2[i, at, :] for i in range(terms * bands8)], axis=0)
            high, low = split(column)
            upper = dot(byt_h[:, : terms * py], high)
            result = upper[:ext] + upper[ext:] + dot(byt_h[:ext, : terms * py], low)
            up_s[z] = halo_code(result[:lead])
            own[z] = result[lead : lead + py]
            dn_s[z] = halo_code(result[lead + py :])
            return carry

        lax.fori_loop(0, cz, back, 0)

        @pl.when(me > 0)
        def _():
            halo(rel, True).start()

        @pl.when(me < blocks - 1)
        def _():
            halo(rel, False).start()

    first = {}
    for rel in range(1, blocks + 1):
        k = lax.rem(me + rel, blocks)
        rows = pl.ds(k * cz, cz)

        @pl.when(me > 0)
        def _():
            remote(dn_s.at[rows], up_r.at[rows], sh.at[k, 1], rh.at[k, 1], (grp, me - 1)).wait_recv()
            own[rows, 0:lead, :] = own[rows, 0:lead, :] + halo_of(up_r[rows])

        @pl.when(me < blocks - 1)
        def _():
            remote(up_s.at[rows], dn_r.at[rows], sh.at[k, 0], rh.at[k, 0], (grp, me + 1)).wait_recv()
            own[rows, py - lead : py, :] = own[rows, py - lead : py, :] + halo_of(dn_r[rows])

        value = jnp.log(own[rows])
        own[rows] = value
        logs_s[rows] = log_code(value)
        for q in range(1, groups):
            peer = lax.rem(grp + q, groups)
            copy = remote(logs_s.at[k * cz + peer], logs_r.at[rel - 1, q - 1], s1.at[rel - 1, q - 1], r1.at[rel - 1, q - 1], (peer, me))
            copy.start()
            first[rel, q] = copy

    for rel in range(1, blocks + 1):
        k = lax.rem(me + rel, blocks)
        total = own[k * cz + grp]
        for q in range(1, groups):
            first[rel, q].wait_recv()
            total = total + log_of(logs_r[rel - 1, q - 1])
        code = log_code(total * (1.0 / groups))
        if rel == blocks:
            lout[grp, me] = code
        else:
            mean_s[rel] = code
            copy = remote(mean_s.at[rel], lout.at[grp, me], s2.at[rel], r2.at[rel], (grp, k))
            copy.start()
            sends.append(copy)

    for rel in [0] + list(range(1, blocks)):
        src = lax.rem(me + blocks - rel, blocks)
        here = lout.at[grp, src]
        if rel > 0:
            remote(here, here, s2.at[rel], r2.at[rel], (grp, src)).wait_recv()
        for q in range(1, groups):
            copy = remote(here, here, s3.at[rel, q - 1], r3.at[rel, q - 1], (lax.rem(grp + q, groups), me))
            copy.start()
            sends.append(copy)

    for rel in range(1, blocks + 1):
        @pl.when(me > 0)
        def _():
            halo(rel, True).wait_send()

        @pl.when(me < blocks - 1)
        def _():
            halo(rel, False).wait_send()
    for copy in sends:
        copy.wait_send()
    for copy in first.values():
        copy.wait_send()
    for rel in [0] + list(range(1, blocks)):
        src = lax.rem(me + blocks - rel, blocks)
        for q in range(1, groups):
            peer = lax.rem(grp + groups - q, groups)
            theirs = lout.at[peer, src]
            remote(theirs, theirs, s3.at[rel, q - 1], r3.at[rel, q - 1], (peer, me)).wait_recv()


def fused(estimate, measured, tile_plane, tile_strip, view_group, kernel_cols, kernel_rows, kernel_planes):
    cz, ny, nx = estimate.shape
    blocks = lax.axis_size("blk")
    groups = lax.axis_size("grp")
    nz = cz * blocks
    py = ny // blocks
    ranks, width = kernel_rows.shape[1:]
    lead = -(-(width // 2) // 16) * 16
    ext = py + 2 * lead
    tiles = measured.shape[1]
    per = tiles // blocks
    terms = VSLOT * ranks
    bands8 = py // 8
    wide = 8 * nz
    vmem = pl.BlockSpec(memory_space=pltpu.VMEM)
    smem = pl.BlockSpec(memory_space=pltpu.SMEM)
    anym = pl.BlockSpec(memory_space=pl.ANY)
    dma = pltpu.SemaphoreType.DMA
    order, chosen, weights, table = pl.pallas_call(
        lambda *refs: prep_kernel(per, *refs),
        out_shape=[
            jax.ShapeDtypeStruct((VSLOT, tiles), jnp.int32),
            jax.ShapeDtypeStruct((VSLOT,), jnp.int32),
            jax.ShapeDtypeStruct((VSLOT,), jnp.float32),
            jax.ShapeDtypeStruct((blocks, VSLOT * per, 128), jnp.int32),
        ],
        in_specs=[smem] * 3,
        out_specs=[smem, smem, smem, vmem],
        scratch_shapes=[pltpu.SMEM((blocks,), jnp.int32)],
        name="prep",
    )(view_group, tile_plane, tile_strip)
    f32, b16, i16 = jnp.float32, jnp.bfloat16, jnp.int16
    square = pltpu.VMEM((terms, nx, nx), b16)
    cube = pltpu.VMEM((terms, wide, wide), b16)
    field = pltpu.VMEM((terms * bands8, wide, nx), b16)
    lout = pl.pallas_call(
        lambda *refs: fused_kernel(blocks, groups, lead, *refs),
        out_shape=jax.ShapeDtypeStruct((cz, blocks, py, nx), i16),
        in_specs=[smem, smem, smem, vmem, vmem, anym, vmem, vmem, vmem],
        out_specs=vmem,
        scratch_shapes=[
            pltpu.VMEM(measured.shape, b16),
            pltpu.VMEM((cz, ny + 2 * lead, nx), i16),
            pltpu.VMEM((nz, ext, nx), i16),
            pltpu.VMEM((blocks, VSLOT * per, py, nx), b16),
            pltpu.VMEM((blocks, VSLOT * per, py, nx), b16),
            pltpu.VMEM((blocks, VSLOT * per, 128), jnp.int32),
            pltpu.VMEM((8, 128 * -(-(2 * nx) // 128)), f32),
            square, square, square, square,
            cube, cube, cube, cube,
            pltpu.VMEM((terms * py, 3 * ext), b16),
            pltpu.VMEM((2 * ext, 256), b16),
            pltpu.VMEM((8, 128), b16),
            pltpu.VMEM((256, 128), f32),
            pltpu.VMEM((wide, 128), jnp.int32),
            field, field, field, field,
            pltpu.VMEM((VSLOT * bands8, wide, nx), f32),
            pltpu.VMEM((VSLOT * bands8, wide, nx), f32),
            pltpu.VMEM((terms * bands8, wide, nx), f32),
            pltpu.VMEM((nz, py, nx), f32),
            pltpu.VMEM((nz, lead, nx), i16),
            pltpu.VMEM((nz, lead, nx), i16),
            pltpu.VMEM((nz, lead, nx), i16),
            pltpu.VMEM((nz, lead, nx), i16),
            pltpu.VMEM((nz, py, nx), i16),
            pltpu.VMEM((blocks, groups - 1, py, nx), i16),
            pltpu.VMEM((blocks, py, nx), i16),
            dma,
            dma((blocks,)), dma((blocks,)),
            dma((blocks, groups - 1)), dma((blocks, groups - 1)),
            dma((blocks,)), dma((blocks,)),
            dma((blocks,)), dma((blocks,)),
            dma((blocks, 2)), dma((blocks, 2)),
            dma((blocks, groups - 1)), dma((blocks, groups - 1)),
            dma((blocks,)), dma((blocks,)),
            dma((blocks, groups - 1)), dma((blocks, groups - 1)),
        ],
        compiler_params=pltpu.CompilerParams(collective_id=2, has_side_effects=True, vmem_limit_bytes=60 * 2**20),
        name="fused",
    )(order, chosen, weights, table, estimate, measured, kernel_cols, kernel_rows, kernel_planes)
    mean = log_of(lout.reshape(cz, ny, nx))
    return estimate * jnp.exp(mean)


def shards(estimate, measured, tile_plane, tile_strip, view_group, kernel_cols, kernel_rows, kernel_planes):
    cz, ny, nx = estimate.shape
    blocks = lax.axis_size("blk")
    groups = lax.axis_size("grp")
    py = ny // blocks
    half = kernel_rows.shape[-1] // 2
    lead = -(-half // 16) * 16
    fits = (
        cz == groups
        and cz % 2 == 0
        and blocks > 1
        and py % 16 == 0
        and py >= lead
        and py + 2 * lead <= 128
        and measured.shape[2] == py
        and nx % 128 == 0
        and VSLOT * (measured.shape[1] // blocks) <= 8
        and VSLOT * kernel_rows.shape[1] * py <= 256
        and (8 * cz * blocks) % 128 == 0
        and cz * blocks <= 64
    )
    program = fused if fits else general
    return program(estimate, measured, tile_plane, tile_strip, view_group, kernel_cols, kernel_rows, kernel_planes)


def solution(mesh):
    in_specs = (
        P("blk", None, None),
        P(None, "blk", None, None),
        P(None, "blk"),
        P(None, "blk"),
        P(),
        P(),
        P(),
        P(),
    )
    return jax.shard_map(
        shards, mesh=mesh, in_specs=in_specs, out_specs=P("blk", None, None), check_vma=False
    )
```

```python
import jax
import jax.numpy as jnp
from jax import lax
from jax.experimental import pallas as pl
from jax.experimental.pallas import tpu as pltpu
from jax.sharding import PartitionSpec as P

VSLOT = 2
HIGH = lax.Precision.HIGH


MESH = pl.DeviceIdType.MESH


def band_kernel(*refs):
    count = len(refs) // 2
    for row, out in zip(refs[:count], refs[count:]):
        number, rows, cols = out.shape
        for n in range(number):
            wide = jnp.broadcast_to(row[n], (rows, row.shape[-1]))
            wide = pltpu.roll(wide, 0, 1, stride=1, stride_axis=0)
            out[n] = wide[:, :cols]


def bands(shapes):
    rows_in, outs = [], []
    for taps, rows, cols, lead in shapes:
        number, width = taps.shape
        half = width // 2
        span = -(-(max(cols, rows) + lead + width) // 128) * 128
        row = jnp.pad(taps, ((0, 0), (0, span - width)))
        row = jnp.roll(row, lead - half, axis=1)
        rows_in.append(row[:, None, :])
        outs.append(jax.ShapeDtypeStruct((number, rows, cols), jnp.float32))
    vmem = pl.BlockSpec(memory_space=pltpu.VMEM)
    return pl.pallas_call(
        band_kernel,
        out_shape=outs,
        in_specs=[vmem] * len(outs),
        out_specs=[vmem] * len(outs),
    )(*rows_in)


def spread_kernel(blocks, groups, step, padded, planes, tiles, pencil, got, arrived, sa, ra, sb, rb, sp, rp, st, rt):
    me = lax.axis_index("blk")
    grp = lax.axis_index("grp")
    cz, span = pencil.shape[1], pencil.shape[2]
    cq = cz // groups
    mine = pl.ds(grp * cq, cq)
    barrier = pltpu.get_barrier_semaphore()
    for k in range(1, groups):
        pl.semaphore_signal(barrier, inc=1, device_id=(lax.rem(grp + k, groups), me), device_id_type=MESH)
    for rel in range(1, blocks):
        pl.semaphore_signal(barrier, inc=1, device_id=(grp, lax.rem(me + rel, blocks)), device_id_type=MESH)
    pl.semaphore_wait(barrier, groups + blocks - 2)

    first, small, second, large = {}, {}, {}, {}
    for rel in range(1, blocks):
        dest = lax.rem(me + rel, blocks)
        first[rel] = pltpu.make_async_remote_copy(
            src_ref=padded.at[mine, pl.ds(dest * step, span)],
            dst_ref=pencil.at[me, mine],
            send_sem=sa.at[rel],
            recv_sem=ra.at[rel],
            device_id=(grp, dest),
            device_id_type=MESH,
        )
        first[rel].start()
    for rel in range(1, blocks):
        dest = lax.rem(me + rel, blocks)
        small[rel] = pltpu.make_async_remote_copy(
            src_ref=planes.at[dest],
            dst_ref=got.at[me],
            send_sem=sp.at[rel],
            recv_sem=rp.at[rel],
            device_id=(grp, dest),
            device_id_type=MESH,
        )
        small[rel].start()
    for rel in range(1, blocks):
        dest = lax.rem(me + rel, blocks)
        large[rel] = pltpu.make_async_remote_copy(
            src_ref=tiles.at[dest],
            dst_ref=arrived.at[me],
            send_sem=st.at[rel],
            recv_sem=rt.at[rel],
            device_id=(grp, dest),
            device_id_type=MESH,
        )
        large[rel].start()
    arrived[me] = tiles[me]
    pencil[me] = padded[:, pl.ds(me * step, span)]
    got[me] = planes[me]
    for rel in range(1, blocks):
        src = lax.rem(me + blocks - rel, blocks)
        landed = pencil.at[src, mine]
        pltpu.make_async_remote_copy(
            src_ref=landed,
            dst_ref=landed,
            send_sem=sa.at[rel],
            recv_sem=ra.at[rel],
            device_id=(grp, src),
            device_id_type=MESH,
        ).wait_recv()
        for k in range(1, groups):
            second[rel, k] = pltpu.make_async_remote_copy(
                src_ref=landed,
                dst_ref=landed,
                send_sem=sb.at[rel, k - 1],
                recv_sem=rb.at[rel, k - 1],
                device_id=(lax.rem(grp + k, groups), me),
                device_id_type=MESH,
            )
            second[rel, k].start()
    for rel in range(1, blocks):
        src = lax.rem(me + blocks - rel, blocks)
        for k in range(1, groups):
            peer = lax.rem(grp + groups - k, groups)
            theirs = pencil.at[src, pl.ds(peer * cq, cq)]
            pltpu.make_async_remote_copy(
                src_ref=theirs,
                dst_ref=theirs,
                send_sem=sb.at[rel, k - 1],
                recv_sem=rb.at[rel, k - 1],
                device_id=(peer, me),
                device_id_type=MESH,
            ).wait_recv()
        pltpu.make_async_remote_copy(
            src_ref=planes.at[src],
            dst_ref=got.at[src],
            send_sem=sp.at[rel],
            recv_sem=rp.at[rel],
            device_id=(grp, src),
            device_id_type=MESH,
        ).wait_recv()
        pltpu.make_async_remote_copy(
            src_ref=tiles.at[src],
            dst_ref=arrived.at[src],
            send_sem=st.at[rel],
            recv_sem=rt.at[rel],
            device_id=(grp, src),
            device_id_type=MESH,
        ).wait_recv()
    for copies in (first, small, second, large):
        for copy in copies.values():
            copy.wait_send()


def spread(estimate, planes, tiles, lead, blocks, groups):
    cz, ny, nx = estimate.shape
    py = ny // blocks
    chunk = min(py, lead)
    span = (py + 2 * lead) // chunk
    padded = jnp.pad(estimate, ((0, 0), (lead, lead), (0, 0))).reshape(cz, -1, chunk, nx)
    vmem = pl.BlockSpec(memory_space=pltpu.VMEM)
    dma = pltpu.SemaphoreType.DMA
    pencil, got, arrived = pl.pallas_call(
        lambda *refs: spread_kernel(blocks, groups, py // chunk, *refs),
        out_shape=[
            jax.ShapeDtypeStruct((blocks, cz, span, chunk, nx), jnp.float32),
            jax.ShapeDtypeStruct(planes.shape, jnp.int32),
            jax.ShapeDtypeStruct(tiles.shape, tiles.dtype),
        ],
        in_specs=[vmem] * 3,
        out_specs=[vmem] * 3,
        scratch_shapes=[
            dma((blocks,)),
            dma((blocks,)),
            dma((blocks, groups - 1)),
            dma((blocks, groups - 1)),
            dma((blocks,)),
            dma((blocks,)),
            dma((blocks,)),
            dma((blocks,)),
        ],
        compiler_params=pltpu.CompilerParams(collective_id=1, has_side_effects=True),
        cost_estimate=pl.CostEstimate(flops=0, bytes_accessed=1 << 26, transcendentals=0),
        name="spread",
    )(padded, planes, tiles)
    return pencil.reshape(cz * blocks, py + 2 * lead, nx), got, arrived


def finish_kernel(blocks, groups, logs, est, out, got1, send2, got2, s1, r1, s2, r2, s3, r3):
    me = lax.axis_index("blk")
    grp = lax.axis_index("grp")
    cq = est.shape[0] // groups
    mine = pl.ds(grp * cq, cq)
    barrier = pltpu.get_barrier_semaphore()
    for k in range(1, groups):
        pl.semaphore_signal(barrier, inc=1, device_id=(lax.rem(grp + k, groups), me), device_id_type=MESH)
    for rel in range(1, blocks):
        pl.semaphore_signal(barrier, inc=1, device_id=(grp, lax.rem(me + rel, blocks)), device_id_type=MESH)
    pl.semaphore_wait(barrier, groups + blocks - 2)
    order = list(range(1, blocks)) + [0]

    first, second, third = {}, {}, {}
    for rel in order:
        dest = lax.rem(me + rel, blocks)
        for k in range(1, groups):
            peer = lax.rem(grp + k, groups)
            first[rel, k] = pltpu.make_async_remote_copy(
                src_ref=logs.at[dest, pl.ds(peer * cq, cq)],
                dst_ref=got1.at[rel, k - 1],
                send_sem=s1.at[rel, k - 1],
                recv_sem=r1.at[rel, k - 1],
                device_id=(peer, me),
                device_id_type=MESH,
            )
            first[rel, k].start()
    for rel in order:
        dest = lax.rem(me + rel, blocks)
        total = logs[dest, mine]
        for k in range(1, groups):
            first[rel, k].wait_recv()
            total = total + got1[rel, k - 1]
        if rel == 0:
            got2[0] = total
        else:
            send2[rel] = total
            second[rel] = pltpu.make_async_remote_copy(
                src_ref=send2.at[rel],
                dst_ref=got2.at[rel],
                send_sem=s2.at[rel],
                recv_sem=r2.at[rel],
                device_id=(grp, dest),
                device_id_type=MESH,
            )
            second[rel].start()
    for rel in order:
        strip = lax.rem(me + blocks - rel, blocks)
        if rel != 0:
            second[rel].wait_recv()
        out[mine, strip] = est[mine, strip] * jnp.exp(got2[rel] * (1.0 / groups))
        for k in range(1, groups):
            third[rel, k] = pltpu.make_async_remote_copy(
                src_ref=out.at[mine, strip],
                dst_ref=out.at[mine, strip],
                send_sem=s3.at[rel, k - 1],
                recv_sem=r3.at[rel, k - 1],
                device_id=(lax.rem(grp + k, groups), me),
                device_id_type=MESH,
            )
            third[rel, k].start()
    for copy in first.values():
        copy.wait_send()
    for copy in second.values():
        copy.wait_send()
    for copy in third.values():
        copy.wait_send()
    for rel in order:
        strip = lax.rem(me + blocks - rel, blocks)
        for k in range(1, groups):
            peer = lax.rem(grp + groups - k, groups)
            theirs = out.at[pl.ds(peer * cq, cq), strip]
            pltpu.make_async_remote_copy(
                src_ref=theirs,
                dst_ref=theirs,
                send_sem=s3.at[rel, k - 1],
                recv_sem=r3.at[rel, k - 1],
                device_id=(peer, me),
                device_id_type=MESH,
            ).wait_recv()


def finish(logs, estimate, blocks, groups):
    cz, ny, nx = estimate.shape
    py = ny // blocks
    cq = cz // groups
    vmem = pl.BlockSpec(memory_space=pltpu.VMEM)
    dma = pltpu.SemaphoreType.DMA
    out = pl.pallas_call(
        lambda *refs: finish_kernel(blocks, groups, *refs),
        out_shape=jax.ShapeDtypeStruct((cz, blocks, py, nx), jnp.float32),
        in_specs=[vmem, vmem],
        out_specs=vmem,
        scratch_shapes=[
            pltpu.VMEM((blocks, groups - 1, cq, py, nx), jnp.float32),
            pltpu.VMEM((blocks, cq, py, nx), jnp.float32),
            pltpu.VMEM((blocks, cq, py, nx), jnp.float32),
            dma((blocks, groups - 1)),
            dma((blocks, groups - 1)),
            dma((blocks,)),
            dma((blocks,)),
            dma((blocks, groups - 1)),
            dma((blocks, groups - 1)),
        ],
        compiler_params=pltpu.CompilerParams(collective_id=0, has_side_effects=True),
        name="finish",
    )(logs.reshape(blocks, cz, py, nx), estimate.reshape(cz, blocks, py, nx))
    return out.reshape(cz, ny, nx)


def general(estimate, measured, tile_plane, tile_strip, view_group, kernel_cols, kernel_rows, kernel_planes):
    cz, ny, nx = estimate.shape
    blocks = lax.axis_size("blk")
    groups = lax.axis_size("grp")
    nz = cz * blocks
    py = ny // blocks
    half = kernel_rows.shape[-1] // 2
    lead = -(-half // 8) * 8
    ext = py + 2 * lead
    tiles = measured.shape[1]
    per = tiles // blocks

    matches = (view_group == lax.axis_index("grp")).astype(jnp.int32)
    members = jnp.sum(matches).astype(jnp.float32)
    ids = jnp.arange(view_group.shape[0], dtype=jnp.int32)
    ranking = jnp.sum(jnp.where(ids[None, :] < ids[:, None], matches[None, :], 0), axis=1)
    picked = [matches * (ranking == s).astype(jnp.int32) for s in range(VSLOT)]
    chosen = [jnp.sum(p * ids) for p in picked]
    weights = jnp.stack([jnp.sum(p).astype(jnp.float32) / members for p in picked])

    pick = lambda a: jnp.stack([lax.dynamic_index_in_dim(a, c, 0, keepdims=False) for c in chosen])
    pieces, planes, strips = pick(measured), pick(tile_plane), pick(tile_strip)
    number = jnp.arange(tiles, dtype=jnp.int32)
    earlier = (strips[:, :, None] == strips[:, None, :]) & (number[None, :] < number[:, None])
    positions = strips * per + jnp.sum(earlier.astype(jnp.int32), axis=2)
    order = positions[:, None, :] == jnp.arange(tiles, dtype=jnp.int32)[None, :, None]
    send_planes = jnp.sum(jnp.where(order, planes[:, None, :], 0), axis=2)
    send = jnp.einsum("vpi,viyx->pvyx", order.astype(jnp.bfloat16), pieces)
    send = send.reshape(blocks, per, VSLOT, py, nx)

    table = send_planes.reshape(VSLOT, blocks, per).transpose(1, 0, 2)
    table = jnp.pad(table, ((0, 0), (0, 8 - VSLOT), (0, 128 - per)))
    pencil, table, got = spread(estimate, table, send, lead, blocks, groups)
    got = got.reshape(tiles, VSLOT, py, nx)
    got_planes = table[:, :VSLOT, :per].transpose(0, 2, 1).reshape(tiles, VSLOT)
    place = (got_planes[None] == jnp.arange(nz, dtype=jnp.int32)[:, None, None]).astype(jnp.bfloat16)
    observed = jnp.einsum("ptv,tvyx->vpyx", place, got).astype(jnp.float32)

    kc, kr, kp = pick(kernel_cols), pick(kernel_rows), pick(kernel_planes)
    flat = lambda k: k.reshape(-1, k.shape[-1])
    fold = lambda m: m.reshape((VSLOT, -1) + m.shape[1:])
    bx, by, bz = map(fold, bands([(flat(kc), nx, nx, 0), (flat(kr), py, ext, lead), (flat(kp), nz, nz, 0)]))
    byw = by * weights[:, None, None, None]

    t = jnp.einsum("zmx,vrim->vrzix", pencil, by, precision=HIGH)
    t = jnp.einsum("vrzix,vrnx->vrzin", t, bx, precision=HIGH)
    blurred = jnp.einsum("vrzin,vrpz->vpin", t, bz, precision=HIGH)
    ratios = observed / blurred
    a = jnp.einsum("vpin,vrpz->vrzin", ratios, bz, precision=HIGH)
    a = jnp.einsum("vrzin,vrnx->vrzix", a, bx, precision=HIGH)
    wide = jnp.einsum("vrzix,vrim->zmx", a, byw, precision=HIGH)

    chunk = min(py, lead)
    average = wide[:, lead : lead + py]
    for d in range(1, lead // chunk + 1):
        up = wide[:, lead + py + (d - 1) * chunk : lead + py + d * chunk]
        down = wide[:, lead - d * chunk : lead - (d - 1) * chunk]
        up = lax.ppermute(up, "blk", [(i, i + d) for i in range(blocks - d)])
        down = lax.ppermute(down, "blk", [(i, i - d) for i in range(d, blocks)])
        rest = py - chunk
        average = average + jnp.pad(up, ((0, 0), (0, rest), (0, 0))) + jnp.pad(down, ((0, 0), (rest, 0), (0, 0)))
    logs = jnp.log(average)
    return finish(logs, estimate, blocks, groups)


def split(value):
    high = value.astype(jnp.bfloat16)
    low = (value - high.astype(jnp.float32)).astype(jnp.bfloat16)
    return high, low


def dot(a, b):
    return jnp.dot(a, b, preferred_element_type=jnp.float32)


def dot3(a, b):
    return dot(jnp.concatenate([a[0], a[1], a[0]], axis=1), jnp.concatenate([b[0], b[0], b[1]], axis=0))


EST = 16383.0
HALO = 65534.0
LOG = 32767.0
KNEE = 4.0


def to_code(value):
    return ((value + 0.5).astype(jnp.int32) - 32768).astype(jnp.int16)


def log_code(logs):
    return to_code(logs / (KNEE + jnp.abs(logs)) * LOG + 32768.0)


def log_of(code):
    value = code.astype(jnp.int32).astype(jnp.float32) * (1.0 / LOG)
    return KNEE * value / (1.0 - jnp.abs(value))


def halo_code(value):
    return to_code(value / (1.0 + value) * HALO)


def halo_of(code):
    value = (code.astype(jnp.int32) + 32768).astype(jnp.float32) * (1.0 / HALO)
    return value / (1.0 - value)


def fused_kernel(
    blocks, groups, lead,
    view_group, tile_plane, tile_strip, est, measured, kc, kr, kp,
    lout,
    stage, ecode, pencil, table, sendt, arrived, got, rowbuf,
    bxt_h, bxt_l, bx_h, bx_l, kz_h, kz_l, kzt_h, kzt_l, byf, byt, byw, pk,
    t1_h, t1_l, t2_h, t2_l, rat_h, rat_l, blur, obs, a2, own, up_s, dn_s, up_r, dn_r, logs_s, logs_r, mean_s,
    sm, sa, ra, sb, rb, sp, rp, st, rt, sh, rh, s1, r1, s2, r2, s3, r3,
):
    me = lax.axis_index("blk")
    grp = lax.axis_index("grp")
    cz, ny, nx = est.shape
    views, tiles = tile_plane.shape
    py = ny // blocks
    nz = cz * blocks
    ext = py + 2 * lead
    ranks, width = kc.shape[1], kc.shape[2]
    half = width // 2
    terms = VSLOT * ranks
    per = tiles // blocks
    bands8 = py // 8
    parts = py // 16
    wide = 8 * nz
    chunk = 8 * cz
    steps = blocks // 2

    def remote(src, dst, send, recv, to):
        return pltpu.make_async_remote_copy(
            src_ref=src, dst_ref=dst, send_sem=send, recv_sem=recv, device_id=to, device_id_type=MESH
        )

    def source(rel):
        return lax.rem(me + blocks - rel, blocks)

    def strip(index):
        return pl.ds(pl.multiple_of(index * py, py), py)

    load = pltpu.make_async_copy(measured, stage, sm)
    load.start()
    barrier = pltpu.get_barrier_semaphore()
    for k in range(1, groups):
        pl.semaphore_signal(barrier, inc=1, device_id=(lax.rem(grp + k, groups), me), device_id_type=MESH)
    for rel in range(1, blocks):
        pl.semaphore_signal(barrier, inc=1, device_id=(grp, lax.rem(me + rel, blocks)), device_id_type=MESH)

    for c in range(cz):
        ecode[c, 0:lead, :] = jnp.full((lead, nx), -32768, jnp.int16)
        ecode[c, lead + ny : lead + ny + lead, :] = jnp.full((lead, nx), -32768, jnp.int16)
        ecode[c, lead : lead + ny, :] = to_code(est[c] * EST)
    pl.semaphore_wait(barrier, groups + blocks - 2)

    sends = []
    for rel in range(1, blocks):
        dest = lax.rem(me + rel, blocks)
        copy = remote(
            ecode.at[grp, pl.ds(pl.multiple_of(dest * py, py), ext)],
            pencil.at[me * cz + grp],
            sa.at[rel], ra.at[rel], (grp, dest),
        )
        copy.start()
        sends.append(copy)

    total, first, second = jnp.int32(0), jnp.int32(0), jnp.int32(0)
    for view in range(views):
        match = view_group[view] == grp
        first = jnp.where(match & (total == 0), view, first)
        second = jnp.where(match & (total == 1), view, second)
        total = total + match.astype(jnp.int32)
    single = total < VSLOT
    chosen = (first, jnp.where(single, first, second))
    weights = (jnp.where(single, 1.0, 1.0 / VSLOT), jnp.where(single, 0.0, 1.0 / VSLOT))
    bits = (tiles - 1).bit_length()
    order = []
    for slot in range(VSLOT):
        packed = [jnp.int32(0)] * blocks
        for tile in range(tiles):
            where = tile_strip[chosen[slot], tile]
            packed = [jnp.where(where == d, (p << bits) + tile, p) for d, p in enumerate(packed)]
        order.append([[(p >> (bits * j)) & ((1 << bits) - 1) for j in range(per)] for p in packed])
    for d in range(blocks):
        for slot in range(VSLOT):
            for j in range(per):
                plane = tile_plane[chosen[slot], order[slot][d][j]]
                table[d, slot * per + j : slot * per + j + 1, :] = jnp.full((1, 128), plane, jnp.int32)
    for rel in range(1, blocks):
        dest = lax.rem(me + rel, blocks)
        copy = remote(table.at[dest], got.at[me], sp.at[rel], rp.at[rel], (grp, dest))
        copy.start()
        sends.append(copy)
    load.wait()
    for part in range(parts):
        for d in range(blocks):
            for slot in range(VSLOT):
                for j in range(per):
                    sendt[part, d, slot * per + j] = stage[chosen[slot], order[slot][d][j], 16 * part : 16 * part + 16, :]
        for rel in range(1, blocks):
            dest = lax.rem(me + rel, blocks)
            copy = remote(
                sendt.at[part, dest], arrived.at[part, me], st.at[part, rel], rt.at[part, rel], (grp, dest)
            )
            copy.start()
            sends.append(copy)
        arrived[part, me] = sendt[part, me]
    got[me] = table[me]
    for c in range(cz):
        pencil[me * cz + c] = ecode[c, pl.ds(pl.multiple_of(me * py, py), ext), :]

    def row_of(taps, view):
        rowbuf[...] = jnp.zeros_like(rowbuf)
        rowbuf[0:ranks, 0:width] = taps[view]

    span = rowbuf.shape[1]
    for slot in range(VSLOT):
        view = chosen[slot]
        row_of(kc, view)
        for r in range(ranks):
            t = slot * ranks + r
            line = jnp.broadcast_to(rowbuf[r : r + 1, :], (nx, span))
            band = pltpu.roll(line, span - half, 1, stride=1, stride_axis=0)[:, :nx]
            bx_h[t], bx_l[t] = split(band)
            bxt_h[t], bxt_l[t] = split(band.T)
        row_of(kr, view)
        for r in range(ranks):
            t = slot * ranks + r
            line = jnp.broadcast_to(rowbuf[r : r + 1, 0:128], (py, 128))
            band = pltpu.roll(line, lead - half, 1, stride=1, stride_axis=0)
            byw[t * py : (t + 1) * py, :] = band * weights[slot]
            high, low = split(band[:, :ext] * (1.0 / EST))
            high, low = high.astype(jnp.float32), low.astype(jnp.float32)
            byf[t * py : (t + 1) * py, :] = jnp.concatenate([high * 256.0, high, low * 256.0], axis=1).astype(jnp.bfloat16)
        row_of(kp, view)
        spread8 = lax.broadcasted_iota(jnp.int32, (128, wide), 1) // 8
        spread8 = (spread8 == lax.broadcasted_iota(jnp.int32, (128, wide), 0)).astype(jnp.bfloat16)
        taps = rowbuf[:, 0:128]
        p0 = taps.astype(jnp.bfloat16)
        rest = taps - p0.astype(jnp.float32)
        p1, p2 = split(rest)
        line8 = dot(p0, spread8) + dot(p1, spread8) + dot(p2, spread8)
        line8 = jnp.concatenate([line8, jnp.zeros_like(line8)], axis=1)
        for r in range(ranks):
            t = slot * ranks + r
            line = jnp.broadcast_to(line8[r : r + 1, :], (nz, 2 * wide))
            band = pltpu.roll(line, 2 * wide - 8 * half, 1, stride=8, stride_axis=0)[:, :wide]
            blur[t, 0:nz, :] = band
    turned = byw[...].T[0:ext, 0 : terms * py]
    high, low = split(turned)
    byt[0:ext, :] = high
    byt[ext : 2 * ext, :] = low

    for rel in range(1, blocks):
        src = source(rel)
        remote(table.at[src], got.at[src], sp.at[rel], rp.at[rel], (grp, src)).wait_recv()
    for slot in range(VSLOT):
        for src in range(blocks):
            for j in range(per):
                tile = src * per + j
                pk[8 * tile : 8 * tile + 8, :] = jnp.broadcast_to(got[src, slot * per + j : slot * per + j + 1, :], (8, 128))
        lanes = lax.broadcasted_iota(jnp.int32, (wide, 128), 1)
        hot = (pk[...] == lanes).astype(jnp.float32).astype(jnp.bfloat16)[:, :nz]
        same = (lax.broadcasted_iota(jnp.int32, (wide, wide), 0) % 8) == (lax.broadcasted_iota(jnp.int32, (wide, wide), 1) % 8)
        for r in range(ranks):
            t = slot * ranks + r
            high, low = split(blur[t, 0:nz, :])
            high = jnp.where(same, dot(hot, high), 0.0)
            low = jnp.where(same, dot(hot, low), 0.0)
            kz_h[t] = high.astype(jnp.bfloat16)
            kz_l[t] = low.astype(jnp.bfloat16)
            for value, ref in ((high.T, kzt_h), (low.T, kzt_l)):
                for k in range(blocks):
                    at = ((k % 2) * steps + k // 2) * chunk
                    ref[t, at : at + chunk, :] = value[k * chunk : (k + 1) * chunk].astype(jnp.bfloat16)

    for rel in range(1, blocks):
        src = source(rel)
        landed = pencil.at[src * cz + grp]
        remote(landed, landed, sa.at[rel], ra.at[rel], (grp, src)).wait_recv()
        for k in range(1, groups):
            copy = remote(landed, landed, sb.at[rel, k - 1], rb.at[rel, k - 1], (lax.rem(grp + k, groups), me))
            copy.start()
            sends.append(copy)

    def blur_rows(src):
        for i in range(cz // 2):
            z = src * cz + 2 * i
            pair = []
            for d in range(2):
                code = pencil[z + d].astype(jnp.int32)
                high = ((code >> 8) + 128).astype(jnp.float32).astype(jnp.bfloat16)
                low = (code & 255).astype(jnp.float32).astype(jnp.bfloat16)
                pair.append(dot(byf[...], jnp.concatenate([high, low, high], axis=0)))
            place = pl.ds(pl.multiple_of(z * 8, 16), 16)
            for t in range(terms):
                for y in range(bands8):
                    at = t * py + 8 * y
                    both = jnp.concatenate([pair[0][at : at + 8], pair[1][at : at + 8]], axis=0)
                    high, low = split(both)
                    t1_h[t * bands8 + y, place, :] = high
                    t1_l[t * bands8 + y, place, :] = low

    def blur_cols(rels):
        places = [pl.ds(pl.multiple_of(source(rel) * chunk, chunk), chunk) for rel in rels]

        def cols(t, carry):
            rows = [(t * bands8 + y, place) for y in range(bands8) for place in places]
            value = dot3(
                (
                    jnp.concatenate([t1_h[y, place, :] for y, place in rows], axis=0),
                    jnp.concatenate([t1_l[y, place, :] for y, place in rows], axis=0),
                ),
                (bxt_h[t], bxt_l[t]),
            )
            high, low = split(value)
            for n, (y, place) in enumerate(rows):
                t2_h[y, place, :] = high[n * chunk : (n + 1) * chunk]
                t2_l[y, place, :] = low[n * chunk : (n + 1) * chunk]
            return carry

        lax.fori_loop(0, terms, cols, 0)

    for rel in range(blocks):
        src = source(rel)
        for k in range(1, groups if rel else 1):
            peer = lax.rem(grp + groups - k, groups)
            theirs = pencil.at[src * cz + peer]
            remote(theirs, theirs, sb.at[rel, k - 1], rb.at[rel, k - 1], (peer, me)).wait_recv()
        blur_rows(src)
        if rel == steps - 1:
            blur_cols(range(steps))
    blur_cols(range(steps, blocks))

    def blur_planes(i, carry):
        slot, y = i // bands8, i % bands8
        total = None
        for r in range(ranks):
            t = slot * ranks + r
            piece = dot3((kz_h[t], kz_l[t]), (t2_h[t * bands8 + y], t2_l[t * bands8 + y]))
            total = piece if total is None else total + piece
        blur[i] = total
        return carry

    lax.fori_loop(0, VSLOT * bands8, blur_planes, 0)

    def take(part):
        for rel in range(blocks):
            src = source(rel)
            if rel > 0:
                here = arrived.at[part, src]
                remote(here, here, st.at[part, rel], rt.at[part, rel], (grp, src)).wait_recv()
            for slot in range(VSLOT):
                for j in range(per):
                    tile = arrived[part, src, slot * per + j].astype(jnp.float32)
                    place = pl.ds(pl.multiple_of((src * per + j) * 8, 8), 8)
                    for e in range(2):
                        obs[slot * bands8 + 2 * part + e, place, :] = tile[8 * e : 8 * e + 8]

    for part in range(parts - 1):
        take(part)

        def early(i, carry):
            slot, y = i // 2, 2 * part + i % 2
            ratio = split(obs[slot * bands8 + y] / blur[slot * bands8 + y])
            for r in range(ranks):
                t = slot * ranks + r
                a1 = split(dot3((kzt_h[t], kzt_l[t]), ratio))
                a2[t * bands8 + y] = dot3(a1, (bx_h[t], bx_l[t]))
            return carry

        lax.fori_loop(0, VSLOT * 2, early, 0)

    take(parts - 1)
    for slot in range(VSLOT):
        for e in range(2):
            at = slot * bands8 + bands8 - 2 + e
            rat_h[2 * slot + e], rat_l[2 * slot + e] = split(obs[at] / blur[at])

    def halo(k, up):
        rows = pl.ds(k * cz, cz)
        if up:
            return remote(up_s.at[rows], dn_r.at[rows], sh.at[k, 0], rh.at[k, 0], (grp, me - 1))
        return remote(dn_s.at[rows], up_r.at[rows], sh.at[k, 1], rh.at[k, 1], (grp, me + 1))

    span = steps * chunk

    def late(odd):
        place = pl.ds(odd * span, span)

        def one(slot, carry):
            for r in range(ranks):
                t = slot * ranks + r
                both = [
                    dot3((kzt_h[t, place, :], kzt_l[t, place, :]), (rat_h[2 * slot + e], rat_l[2 * slot + e]))
                    for e in range(2)
                ]
                a1 = split(jnp.concatenate(both, axis=0))
                value = dot3(a1, (bx_h[t], bx_l[t]))
                for e in range(2):
                    a2[t * bands8 + bands8 - 2 + e, place, :] = value[e * span : (e + 1) * span]
            return carry

        lax.fori_loop(0, VSLOT, one, 0)

    def back(odd):
        def block(n, carry):
            k = 2 * n + odd
            for c in range(cz):
                z = k * cz + c
                at = pl.ds(pl.multiple_of((odd * steps + n) * chunk + 8 * c, 8), 8)
                column = jnp.concatenate([a2[i, at, :] for i in range(terms * bands8)], axis=0)
                high, low = split(column)
                upper = dot(byt[...], high)
                result = upper[:ext] + upper[ext:] + dot(byt[:ext, :], low)
                up_s[z] = halo_code(result[:lead])
                own[z] = result[lead : lead + py]
                dn_s[z] = halo_code(result[lead + py :])

            @pl.when(me > 0)
            def _():
                halo(k, True).start()

            @pl.when(me < blocks - 1)
            def _():
                halo(k, False).start()

            return carry

        lax.fori_loop(0, steps, block, 0)

    first = {}

    def take_halo(odd):
        for n in range(steps):
            k = 2 * n + odd
            rows = pl.ds(k * cz, cz)

            @pl.when(me > 0)
            def _():
                remote(dn_s.at[rows], up_r.at[rows], sh.at[k, 1], rh.at[k, 1], (grp, me - 1)).wait_recv()
                own[rows, 0:lead, :] = own[rows, 0:lead, :] + halo_of(up_r[rows])

            @pl.when(me < blocks - 1)
            def _():
                remote(up_s.at[rows], dn_r.at[rows], sh.at[k, 0], rh.at[k, 0], (grp, me + 1)).wait_recv()
                own[rows, py - lead : py, :] = own[rows, py - lead : py, :] + halo_of(dn_r[rows])

            value = jnp.log(own[rows])
            own[rows] = value
            logs_s[rows] = log_code(value)
            for q in range(1, groups):
                peer = lax.rem(grp + q, groups)
                first[k, q] = remote(
                    logs_s.at[k * cz + peer], logs_r.at[k, q - 1], s1.at[k, q - 1], r1.at[k, q - 1], (peer, me)
                )
                first[k, q].start()

    def mean_out(k):
        return remote(mean_s.at[k], lout.at[grp, strip(me)], s2.at[k], r2.at[me], (grp, k))

    def take_logs(odd):
        for n in range(steps):
            k = 2 * n + odd
            total = own[k * cz + grp]
            for q in range(1, groups):
                first[k, q].wait_recv()
                total = total + log_of(logs_r[k, q - 1])
            mean_s[k] = log_code(total * (1.0 / groups))

            @pl.when(me != k)
            def _():
                mean_out(k).start()

            @pl.when(me == k)
            def _():
                lout[grp, strip(me), :] = mean_s[k]

    def pass_on(src, q):
        here = lout.at[grp, strip(src)]
        return remote(here, here, s3.at[src, q - 1], r3.at[src, q - 1], (lax.rem(grp + q, groups), me))

    def take_mean(odd):
        @pl.when(lax.rem(me, 2) == odd)
        def _():
            for rel in range(blocks):
                src = source(rel)
                here = lout.at[grp, strip(src)]
                if rel > 0:
                    remote(here, here, s2.at[src], r2.at[src], (grp, src)).wait_recv()
                for q in range(1, groups):
                    pass_on(src, q).start()

    late(0)
    back(0)
    late(1)
    take_halo(0)
    back(1)
    take_logs(0)
    take_halo(1)
    take_mean(0)
    take_logs(1)
    take_mean(1)

    for k in range(blocks):
        @pl.when(me > 0)
        def _():
            halo(k, True).wait_send()

        @pl.when(me < blocks - 1)
        def _():
            halo(k, False).wait_send()

        @pl.when(me != k)
        def _():
            mean_out(k).wait_send()

        for q in range(1, groups):
            pass_on(k, q).wait_send()
            first[k, q].wait_send()
    for copy in sends:
        copy.wait_send()
    for rel in range(blocks):
        src = source(rel)
        for q in range(1, groups):
            peer = lax.rem(grp + groups - q, groups)
            theirs = lout.at[peer, strip(src)]
            remote(theirs, theirs, s3.at[src, q - 1], r3.at[src, q - 1], (peer, me)).wait_recv()


def fused(estimate, measured, tile_plane, tile_strip, view_group, kernel_cols, kernel_rows, kernel_planes):
    cz, ny, nx = estimate.shape
    blocks = lax.axis_size("blk")
    groups = lax.axis_size("grp")
    nz = cz * blocks
    py = ny // blocks
    ranks, width = kernel_rows.shape[1:]
    lead = -(-(width // 2) // 16) * 16
    ext = py + 2 * lead
    per = measured.shape[1] // blocks
    terms = VSLOT * ranks
    bands8 = py // 8
    parts = py // 16
    wide = 8 * nz
    vmem = pl.BlockSpec(memory_space=pltpu.VMEM)
    smem = pl.BlockSpec(memory_space=pltpu.SMEM)
    dma = pltpu.SemaphoreType.DMA
    f32, b16, i16, i32 = jnp.float32, jnp.bfloat16, jnp.int16, jnp.int32
    square = pltpu.VMEM((terms, nx, nx), b16)
    cube = pltpu.VMEM((terms, wide, wide), b16)
    field = pltpu.VMEM((terms * bands8, wide, nx), b16)
    ratio = pltpu.VMEM((VSLOT * 2, wide, nx), b16)
    edge = pltpu.VMEM((nz, lead, nx), i16)
    batch = pltpu.VMEM((parts, blocks, VSLOT * per, 16, nx), b16)
    listing = pltpu.VMEM((blocks, VSLOT * per, 128), i32)
    lout = pl.pallas_call(
        lambda *refs: fused_kernel(blocks, groups, lead, *refs),
        out_shape=jax.ShapeDtypeStruct((cz, ny, nx), i16),
        in_specs=[smem, smem, smem, vmem, pl.BlockSpec(memory_space=pl.ANY), vmem, vmem, vmem],
        out_specs=vmem,
        scratch_shapes=[
            pltpu.VMEM(measured.shape, b16),
            pltpu.VMEM((cz, ny + 2 * lead, nx), i16),
            pltpu.VMEM((nz, ext, nx), i16),
            listing,
            batch, batch,
            listing,
            pltpu.VMEM((8, 2 * nx), f32),
            square, square, square, square,
            cube, cube, cube, cube,
            pltpu.VMEM((terms * py, 3 * ext), b16),
            pltpu.VMEM((2 * ext, terms * py), b16),
            pltpu.VMEM((256, 128), f32),
            pltpu.VMEM((wide, 128), i32),
            field, field, field, field,
            ratio, ratio,
            pltpu.VMEM((VSLOT * bands8, wide, nx), f32),
            pltpu.VMEM((VSLOT * bands8, wide, nx), f32),
            pltpu.VMEM((terms * bands8, wide, nx), f32),
            pltpu.VMEM((nz, py, nx), f32),
            edge, edge, edge, edge,
            pltpu.VMEM((nz, py, nx), i16),
            pltpu.VMEM((blocks, groups - 1, py, nx), i16),
            pltpu.VMEM((blocks, py, nx), i16),
            dma,
            dma((blocks,)), dma((blocks,)),
            dma((blocks, groups - 1)), dma((blocks, groups - 1)),
            dma((blocks,)), dma((blocks,)),
            dma((parts, blocks)), dma((parts, blocks)),
            dma((blocks, 2)), dma((blocks, 2)),
            dma((blocks, groups - 1)), dma((blocks, groups - 1)),
            dma((blocks,)), dma((blocks,)),
            dma((blocks, groups - 1)), dma((blocks, groups - 1)),
        ],
        compiler_params=pltpu.CompilerParams(collective_id=2, has_side_effects=True, vmem_limit_bytes=60 * 2**20),
        name="fused",
    )(view_group, tile_plane, tile_strip, estimate, measured, kernel_cols, kernel_rows, kernel_planes)
    return estimate * jnp.exp(log_of(lout))


def shards(estimate, measured, tile_plane, tile_strip, view_group, kernel_cols, kernel_rows, kernel_planes):
    cz, ny, nx = estimate.shape
    blocks = lax.axis_size("blk")
    groups = lax.axis_size("grp")
    py = ny // blocks
    half = kernel_rows.shape[-1] // 2
    lead = -(-half // 16) * 16
    per = measured.shape[1] // blocks
    fits = (
        cz == groups
        and cz % 2 == 0
        and blocks % 2 == 0
        and py % 16 == 0
        and py >= lead
        and py + 2 * lead <= 128
        and measured.shape[2] == py
        and nx % 128 == 0
        and VSLOT * per <= 8
        and VSLOT * kernel_rows.shape[1] * py <= 256
        and per * (measured.shape[1] - 1).bit_length() <= 31
        and (8 * cz * blocks) % 128 == 0
        and cz * blocks <= 64
    )
    program = fused if fits else general
    return program(estimate, measured, tile_plane, tile_strip, view_group, kernel_cols, kernel_rows, kernel_planes)


def solution(mesh):
    in_specs = (
        P("blk", None, None),
        P(None, "blk", None, None),
        P(None, "blk"),
        P(None, "blk"),
        P(),
        P(),
        P(),
        P(),
    )
    return jax.shard_map(
        shards, mesh=mesh, in_specs=in_specs, out_specs=P("blk", None, None), check_vma=False
    )
```

```python
import jax
import jax.numpy as jnp
from jax import lax
from jax.experimental import pallas as pl
from jax.experimental.pallas import tpu as pltpu
from jax.sharding import PartitionSpec as P

VSLOT = 2
HIGH = lax.Precision.HIGH


MESH = pl.DeviceIdType.MESH


def band_kernel(*refs):
    count = len(refs) // 2
    for row, out in zip(refs[:count], refs[count:]):
        number, rows, cols = out.shape
        for n in range(number):
            wide = jnp.broadcast_to(row[n], (rows, row.shape[-1]))
            wide = pltpu.roll(wide, 0, 1, stride=1, stride_axis=0)
            out[n] = wide[:, :cols]


def bands(shapes):
    rows_in, outs = [], []
    for taps, rows, cols, lead in shapes:
        number, width = taps.shape
        half = width // 2
        span = -(-(max(cols, rows) + lead + width) // 128) * 128
        row = jnp.pad(taps, ((0, 0), (0, span - width)))
        row = jnp.roll(row, lead - half, axis=1)
        rows_in.append(row[:, None, :])
        outs.append(jax.ShapeDtypeStruct((number, rows, cols), jnp.float32))
    vmem = pl.BlockSpec(memory_space=pltpu.VMEM)
    return pl.pallas_call(
        band_kernel,
        out_shape=outs,
        in_specs=[vmem] * len(outs),
        out_specs=[vmem] * len(outs),
    )(*rows_in)


def spread_kernel(blocks, groups, step, padded, planes, tiles, pencil, got, arrived, sa, ra, sb, rb, sp, rp, st, rt):
    me = lax.axis_index("blk")
    grp = lax.axis_index("grp")
    cz, span = pencil.shape[1], pencil.shape[2]
    cq = cz // groups
    mine = pl.ds(grp * cq, cq)
    barrier = pltpu.get_barrier_semaphore()
    for k in range(1, groups):
        pl.semaphore_signal(barrier, inc=1, device_id=(lax.rem(grp + k, groups), me), device_id_type=MESH)
    for rel in range(1, blocks):
        pl.semaphore_signal(barrier, inc=1, device_id=(grp, lax.rem(me + rel, blocks)), device_id_type=MESH)
    pl.semaphore_wait(barrier, groups + blocks - 2)

    first, small, second, large = {}, {}, {}, {}
    for rel in range(1, blocks):
        dest = lax.rem(me + rel, blocks)
        first[rel] = pltpu.make_async_remote_copy(
            src_ref=padded.at[mine, pl.ds(dest * step, span)],
            dst_ref=pencil.at[me, mine],
            send_sem=sa.at[rel],
            recv_sem=ra.at[rel],
            device_id=(grp, dest),
            device_id_type=MESH,
        )
        first[rel].start()
    for rel in range(1, blocks):
        dest = lax.rem(me + rel, blocks)
        small[rel] = pltpu.make_async_remote_copy(
            src_ref=planes.at[dest],
            dst_ref=got.at[me],
            send_sem=sp.at[rel],
            recv_sem=rp.at[rel],
            device_id=(grp, dest),
            device_id_type=MESH,
        )
        small[rel].start()
    for rel in range(1, blocks):
        dest = lax.rem(me + rel, blocks)
        large[rel] = pltpu.make_async_remote_copy(
            src_ref=tiles.at[dest],
            dst_ref=arrived.at[me],
            send_sem=st.at[rel],
            recv_sem=rt.at[rel],
            device_id=(grp, dest),
            device_id_type=MESH,
        )
        large[rel].start()
    arrived[me] = tiles[me]
    pencil[me] = padded[:, pl.ds(me * step, span)]
    got[me] = planes[me]
    for rel in range(1, blocks):
        src = lax.rem(me + blocks - rel, blocks)
        landed = pencil.at[src, mine]
        pltpu.make_async_remote_copy(
            src_ref=landed,
            dst_ref=landed,
            send_sem=sa.at[rel],
            recv_sem=ra.at[rel],
            device_id=(grp, src),
            device_id_type=MESH,
        ).wait_recv()
        for k in range(1, groups):
            second[rel, k] = pltpu.make_async_remote_copy(
                src_ref=landed,
                dst_ref=landed,
                send_sem=sb.at[rel, k - 1],
                recv_sem=rb.at[rel, k - 1],
                device_id=(lax.rem(grp + k, groups), me),
                device_id_type=MESH,
            )
            second[rel, k].start()
    for rel in range(1, blocks):
        src = lax.rem(me + blocks - rel, blocks)
        for k in range(1, groups):
            peer = lax.rem(grp + groups - k, groups)
            theirs = pencil.at[src, pl.ds(peer * cq, cq)]
            pltpu.make_async_remote_copy(
                src_ref=theirs,
                dst_ref=theirs,
                send_sem=sb.at[rel, k - 1],
                recv_sem=rb.at[rel, k - 1],
                device_id=(peer, me),
                device_id_type=MESH,
            ).wait_recv()
        pltpu.make_async_remote_copy(
            src_ref=planes.at[src],
            dst_ref=got.at[src],
            send_sem=sp.at[rel],
            recv_sem=rp.at[rel],
            device_id=(grp, src),
            device_id_type=MESH,
        ).wait_recv()
        pltpu.make_async_remote_copy(
            src_ref=tiles.at[src],
            dst_ref=arrived.at[src],
            send_sem=st.at[rel],
            recv_sem=rt.at[rel],
            device_id=(grp, src),
            device_id_type=MESH,
        ).wait_recv()
    for copies in (first, small, second, large):
        for copy in copies.values():
            copy.wait_send()


def spread(estimate, planes, tiles, lead, blocks, groups):
    cz, ny, nx = estimate.shape
    py = ny // blocks
    chunk = min(py, lead)
    span = (py + 2 * lead) // chunk
    padded = jnp.pad(estimate, ((0, 0), (lead, lead), (0, 0))).reshape(cz, -1, chunk, nx)
    vmem = pl.BlockSpec(memory_space=pltpu.VMEM)
    dma = pltpu.SemaphoreType.DMA
    pencil, got, arrived = pl.pallas_call(
        lambda *refs: spread_kernel(blocks, groups, py // chunk, *refs),
        out_shape=[
            jax.ShapeDtypeStruct((blocks, cz, span, chunk, nx), jnp.float32),
            jax.ShapeDtypeStruct(planes.shape, jnp.int32),
            jax.ShapeDtypeStruct(tiles.shape, tiles.dtype),
        ],
        in_specs=[vmem] * 3,
        out_specs=[vmem] * 3,
        scratch_shapes=[
            dma((blocks,)),
            dma((blocks,)),
            dma((blocks, groups - 1)),
            dma((blocks, groups - 1)),
            dma((blocks,)),
            dma((blocks,)),
            dma((blocks,)),
            dma((blocks,)),
        ],
        compiler_params=pltpu.CompilerParams(collective_id=1, has_side_effects=True),
        cost_estimate=pl.CostEstimate(flops=0, bytes_accessed=1 << 26, transcendentals=0),
        name="spread",
    )(padded, planes, tiles)
    return pencil.reshape(cz * blocks, py + 2 * lead, nx), got, arrived


def finish_kernel(blocks, groups, logs, est, out, got1, send2, got2, s1, r1, s2, r2, s3, r3):
    me = lax.axis_index("blk")
    grp = lax.axis_index("grp")
    cq = est.shape[0] // groups
    mine = pl.ds(grp * cq, cq)
    barrier = pltpu.get_barrier_semaphore()
    for k in range(1, groups):
        pl.semaphore_signal(barrier, inc=1, device_id=(lax.rem(grp + k, groups), me), device_id_type=MESH)
    for rel in range(1, blocks):
        pl.semaphore_signal(barrier, inc=1, device_id=(grp, lax.rem(me + rel, blocks)), device_id_type=MESH)
    pl.semaphore_wait(barrier, groups + blocks - 2)
    order = list(range(1, blocks)) + [0]

    first, second, third = {}, {}, {}
    for rel in order:
        dest = lax.rem(me + rel, blocks)
        for k in range(1, groups):
            peer = lax.rem(grp + k, groups)
            first[rel, k] = pltpu.make_async_remote_copy(
                src_ref=logs.at[dest, pl.ds(peer * cq, cq)],
                dst_ref=got1.at[rel, k - 1],
                send_sem=s1.at[rel, k - 1],
                recv_sem=r1.at[rel, k - 1],
                device_id=(peer, me),
                device_id_type=MESH,
            )
            first[rel, k].start()
    for rel in order:
        dest = lax.rem(me + rel, blocks)
        total = logs[dest, mine]
        for k in range(1, groups):
            first[rel, k].wait_recv()
            total = total + got1[rel, k - 1]
        if rel == 0:
            got2[0] = total
        else:
            send2[rel] = total
            second[rel] = pltpu.make_async_remote_copy(
                src_ref=send2.at[rel],
                dst_ref=got2.at[rel],
                send_sem=s2.at[rel],
                recv_sem=r2.at[rel],
                device_id=(grp, dest),
                device_id_type=MESH,
            )
            second[rel].start()
    for rel in order:
        strip = lax.rem(me + blocks - rel, blocks)
        if rel != 0:
            second[rel].wait_recv()
        out[mine, strip] = est[mine, strip] * jnp.exp(got2[rel] * (1.0 / groups))
        for k in range(1, groups):
            third[rel, k] = pltpu.make_async_remote_copy(
                src_ref=out.at[mine, strip],
                dst_ref=out.at[mine, strip],
                send_sem=s3.at[rel, k - 1],
                recv_sem=r3.at[rel, k - 1],
                device_id=(lax.rem(grp + k, groups), me),
                device_id_type=MESH,
            )
            third[rel, k].start()
    for copy in first.values():
        copy.wait_send()
    for copy in second.values():
        copy.wait_send()
    for copy in third.values():
        copy.wait_send()
    for rel in order:
        strip = lax.rem(me + blocks - rel, blocks)
        for k in range(1, groups):
            peer = lax.rem(grp + groups - k, groups)
            theirs = out.at[pl.ds(peer * cq, cq), strip]
            pltpu.make_async_remote_copy(
                src_ref=theirs,
                dst_ref=theirs,
                send_sem=s3.at[rel, k - 1],
                recv_sem=r3.at[rel, k - 1],
                device_id=(peer, me),
                device_id_type=MESH,
            ).wait_recv()


def finish(logs, estimate, blocks, groups):
    cz, ny, nx = estimate.shape
    py = ny // blocks
    cq = cz // groups
    vmem = pl.BlockSpec(memory_space=pltpu.VMEM)
    dma = pltpu.SemaphoreType.DMA
    out = pl.pallas_call(
        lambda *refs: finish_kernel(blocks, groups, *refs),
        out_shape=jax.ShapeDtypeStruct((cz, blocks, py, nx), jnp.float32),
        in_specs=[vmem, vmem],
        out_specs=vmem,
        scratch_shapes=[
            pltpu.VMEM((blocks, groups - 1, cq, py, nx), jnp.float32),
            pltpu.VMEM((blocks, cq, py, nx), jnp.float32),
            pltpu.VMEM((blocks, cq, py, nx), jnp.float32),
            dma((blocks, groups - 1)),
            dma((blocks, groups - 1)),
            dma((blocks,)),
            dma((blocks,)),
            dma((blocks, groups - 1)),
            dma((blocks, groups - 1)),
        ],
        compiler_params=pltpu.CompilerParams(collective_id=0, has_side_effects=True),
        name="finish",
    )(logs.reshape(blocks, cz, py, nx), estimate.reshape(cz, blocks, py, nx))
    return out.reshape(cz, ny, nx)


def general(estimate, measured, tile_plane, tile_strip, view_group, kernel_cols, kernel_rows, kernel_planes):
    cz, ny, nx = estimate.shape
    blocks = lax.axis_size("blk")
    groups = lax.axis_size("grp")
    nz = cz * blocks
    py = ny // blocks
    half = kernel_rows.shape[-1] // 2
    lead = -(-half // 8) * 8
    ext = py + 2 * lead
    tiles = measured.shape[1]
    per = tiles // blocks

    matches = (view_group == lax.axis_index("grp")).astype(jnp.int32)
    members = jnp.sum(matches).astype(jnp.float32)
    ids = jnp.arange(view_group.shape[0], dtype=jnp.int32)
    ranking = jnp.sum(jnp.where(ids[None, :] < ids[:, None], matches[None, :], 0), axis=1)
    picked = [matches * (ranking == s).astype(jnp.int32) for s in range(VSLOT)]
    chosen = [jnp.sum(p * ids) for p in picked]
    weights = jnp.stack([jnp.sum(p).astype(jnp.float32) / members for p in picked])

    pick = lambda a: jnp.stack([lax.dynamic_index_in_dim(a, c, 0, keepdims=False) for c in chosen])
    pieces, planes, strips = pick(measured), pick(tile_plane), pick(tile_strip)
    number = jnp.arange(tiles, dtype=jnp.int32)
    earlier = (strips[:, :, None] == strips[:, None, :]) & (number[None, :] < number[:, None])
    positions = strips * per + jnp.sum(earlier.astype(jnp.int32), axis=2)
    order = positions[:, None, :] == jnp.arange(tiles, dtype=jnp.int32)[None, :, None]
    send_planes = jnp.sum(jnp.where(order, planes[:, None, :], 0), axis=2)
    send = jnp.einsum("vpi,viyx->pvyx", order.astype(jnp.bfloat16), pieces)
    send = send.reshape(blocks, per, VSLOT, py, nx)

    table = send_planes.reshape(VSLOT, blocks, per).transpose(1, 0, 2)
    table = jnp.pad(table, ((0, 0), (0, 8 - VSLOT), (0, 128 - per)))
    pencil, table, got = spread(estimate, table, send, lead, blocks, groups)
    got = got.reshape(tiles, VSLOT, py, nx)
    got_planes = table[:, :VSLOT, :per].transpose(0, 2, 1).reshape(tiles, VSLOT)
    place = (got_planes[None] == jnp.arange(nz, dtype=jnp.int32)[:, None, None]).astype(jnp.bfloat16)
    observed = jnp.einsum("ptv,tvyx->vpyx", place, got).astype(jnp.float32)

    kc, kr, kp = pick(kernel_cols), pick(kernel_rows), pick(kernel_planes)
    flat = lambda k: k.reshape(-1, k.shape[-1])
    fold = lambda m: m.reshape((VSLOT, -1) + m.shape[1:])
    bx, by, bz = map(fold, bands([(flat(kc), nx, nx, 0), (flat(kr), py, ext, lead), (flat(kp), nz, nz, 0)]))
    byw = by * weights[:, None, None, None]

    t = jnp.einsum("zmx,vrim->vrzix", pencil, by, precision=HIGH)
    t = jnp.einsum("vrzix,vrnx->vrzin", t, bx, precision=HIGH)
    blurred = jnp.einsum("vrzin,vrpz->vpin", t, bz, precision=HIGH)
    ratios = observed / blurred
    a = jnp.einsum("vpin,vrpz->vrzin", ratios, bz, precision=HIGH)
    a = jnp.einsum("vrzin,vrnx->vrzix", a, bx, precision=HIGH)
    wide = jnp.einsum("vrzix,vrim->zmx", a, byw, precision=HIGH)

    chunk = min(py, lead)
    average = wide[:, lead : lead + py]
    for d in range(1, lead // chunk + 1):
        up = wide[:, lead + py + (d - 1) * chunk : lead + py + d * chunk]
        down = wide[:, lead - d * chunk : lead - (d - 1) * chunk]
        up = lax.ppermute(up, "blk", [(i, i + d) for i in range(blocks - d)])
        down = lax.ppermute(down, "blk", [(i, i - d) for i in range(d, blocks)])
        rest = py - chunk
        average = average + jnp.pad(up, ((0, 0), (0, rest), (0, 0))) + jnp.pad(down, ((0, 0), (rest, 0), (0, 0)))
    logs = jnp.log(average)
    return finish(logs, estimate, blocks, groups)


def split(value):
    high = value.astype(jnp.bfloat16)
    low = (value - high.astype(jnp.float32)).astype(jnp.bfloat16)
    return high, low


def dot(a, b):
    return jnp.dot(a, b, preferred_element_type=jnp.float32)


def dot3(a, b):
    return dot(jnp.concatenate([a[0], a[1], a[0]], axis=1), jnp.concatenate([b[0], b[0], b[1]], axis=0))


EST = 16383.0
HALO = 65534.0
LOG = 32767.0
KNEE = 4.0


def to_code(value):
    return ((value + 0.5).astype(jnp.int32) - 32768).astype(jnp.int16)


def log_code(logs):
    return to_code(logs / (KNEE + jnp.abs(logs)) * LOG + 32768.0)


def log_of(code):
    value = code.astype(jnp.int32).astype(jnp.float32) * (1.0 / LOG)
    return KNEE * value / (1.0 - jnp.abs(value))


def halo_code(value):
    return to_code(value / (1.0 + value) * HALO)


def halo_of(code):
    value = (code.astype(jnp.int32) + 32768).astype(jnp.float32) * (1.0 / HALO)
    return value / (1.0 - value)


def fused_kernel(
    blocks, groups, lead,
    view_group, tile_plane, tile_strip, estimate, measured, kc, kr, kp,
    lout,
    est, stage, ecode, pencil, table, sendt, arrived, got, rowbuf,
    bxt_h, bxt_l, bx_h, bx_l, kz_h, kz_l, kzt_h, kzt_l, byf, byt, byw, pk,
    t1_h, t1_l, t2_h, t2_l, rat_h, rat_l, blur, obs, a2, own, up_s, dn_s, up_r, dn_r, logs_s, logs_r, mean_s,
    sm, sa, ra, sb, rb, sp, rp, st, rt, sq, rq, sh, rh, s1, r1, s2, r2, s3, r3,
):
    me = lax.axis_index("blk")
    grp = lax.axis_index("grp")
    cz, ny, nx = est.shape
    views, tiles = tile_plane.shape
    py = ny // blocks
    nz = cz * blocks
    ext = py + 2 * lead
    ranks, width = kc.shape[1], kc.shape[2]
    half = width // 2
    terms = VSLOT * ranks
    per = tiles // blocks
    bands8 = py // 8
    parts = py // 16
    wide = 8 * nz
    chunk = 8 * cz
    steps = blocks // 2

    def remote(src, dst, send, recv, to):
        return pltpu.make_async_remote_copy(
            src_ref=src, dst_ref=dst, send_sem=send, recv_sem=recv, device_id=to, device_id_type=MESH
        )

    def source(rel):
        return lax.rem(me + blocks - rel, blocks)

    def strip(index):
        return pl.ds(pl.multiple_of(index * py, py), py)

    double = (grp == 0) | (grp == groups - 1)
    direct = per + per // 2
    fetch = pltpu.make_async_copy(estimate, est, sm.at[0])
    fetch.start()
    load = pltpu.make_async_copy(measured, stage, sm.at[1])
    load.start()
    for part in range(parts):
        arrived[part, :, direct:] = jnp.zeros((blocks, VSLOT * per - direct, 16, nx), jnp.bfloat16)
    barrier = pltpu.get_barrier_semaphore()
    for k in range(1, groups):
        pl.semaphore_signal(barrier, inc=1, device_id=(lax.rem(grp + k, groups), me), device_id_type=MESH)
    for rel in range(1, blocks):
        pl.semaphore_signal(barrier, inc=1, device_id=(grp, lax.rem(me + rel, blocks)), device_id_type=MESH)

    def encode(c):
        ecode[c, 0:lead, :] = jnp.full((lead, nx), -32768, jnp.int16)
        ecode[c, lead + ny : lead + ny + lead, :] = jnp.full((lead, nx), -32768, jnp.int16)
        ecode[c, lead : lead + ny, :] = to_code(est[c] * EST)

    fetch.wait()
    encode(grp)
    pl.semaphore_wait(barrier, groups + blocks - 2)

    sends = []
    for rel in range(1, blocks):
        dest = lax.rem(me + rel, blocks)
        copy = remote(
            ecode.at[grp, pl.ds(pl.multiple_of(dest * py, py), ext)],
            pencil.at[me * cz + grp],
            sa.at[rel], ra.at[rel], (grp, dest),
        )
        copy.start()
        sends.append(copy)

    holds = [jnp.int32(0)] * groups
    doubles, singles = jnp.int32(0), jnp.int32(0)
    for group in range(groups):
        size = jnp.int32(0)
        for view in range(views):
            size = size + (view_group[view] == group).astype(jnp.int32)
        two = size > 1
        column = jnp.where(two, doubles * (groups - 1), 1 + singles)
        doubles = doubles + two.astype(jnp.int32)
        singles = singles + 1 - two.astype(jnp.int32)
        holds = [jnp.where(column == c, group, h) for c, h in enumerate(holds)]
    mine = holds[0]
    for c in range(1, groups):
        mine = jnp.where(grp == c, holds[c], mine)

    def views_of(group):
        low, high = jnp.int32(views), jnp.int32(0)
        for view in range(views):
            match = view_group[view] == group
            low = jnp.where(match, jnp.minimum(low, view), low)
            high = jnp.where(match, view, high)
        return jnp.minimum(low, views - 1), high

    own_views = views_of(mine)
    ends = (views_of(holds[0])[1], views_of(holds[groups - 1])[1])
    chosen = own_views
    listed = (own_views[0], jnp.where(double, own_views[1], ends[0]), jnp.where(double, own_views[1], ends[1]))
    weights = (jnp.where(double, 1.0 / VSLOT, 1.0), jnp.where(double, 1.0 / VSLOT, 0.0))
    bits = (tiles - 1).bit_length()
    order = []
    for slot in range(len(listed)):
        packed = [jnp.int32(0)] * blocks
        for tile in range(tiles):
            where = tile_strip[listed[slot], tile]
            packed = [jnp.where(where == d, (p << bits) + tile, p) for d, p in enumerate(packed)]
        order.append([[(p >> (bits * j)) & ((1 << bits) - 1) for j in range(per)] for p in packed])
    for d in range(blocks):
        for slot in range(VSLOT):
            for j in range(per):
                plane = tile_plane[listed[slot], order[slot][d][j]]
                table[d, slot * per + j : slot * per + j + 1, :] = jnp.full((1, 128), plane, jnp.int32)
    for rel in range(1, blocks):
        dest = lax.rem(me + rel, blocks)
        copy = remote(table.at[dest], got.at[me], sp.at[rel], rp.at[rel], (grp, dest))
        copy.start()
        sends.append(copy)
    load.wait()
    for part in range(parts):
        for d in range(blocks):
            picks = [(listed[0], order[0][d][j]) for j in range(per)]
            for e in range(per // 2):
                one = order[1 + e][d]
                lent = jnp.where(grp == 1, one[per // 2], one[per // 2 + 1])
                picks.append((listed[1 + e], jnp.where(double, one[e], lent)))
            picks += [(listed[1], order[1][d][j]) for j in range(per // 2, per)]
            for e, (view, tile) in enumerate(picks):
                sendt[part, d, e] = stage[view, tile, 16 * part : 16 * part + 16, :]
        for rel in range(1, blocks):
            dest = lax.rem(me + rel, blocks)
            copy = remote(
                sendt.at[part, dest, pl.ds(0, direct)],
                arrived.at[part, me, pl.ds(0, direct)],
                st.at[part, rel], rt.at[part, rel], (grp, dest),
            )
            copy.start()
            sends.append(copy)
        arrived[part, me] = sendt[part, me]
    for rel in range(1, blocks):
        src = source(rel)
        landed = pencil.at[src * cz + grp]
        remote(landed, landed, sa.at[rel], ra.at[rel], (grp, src)).wait_recv()
        for k in range(1, groups):
            copy = remote(landed, landed, sb.at[rel, k - 1], rb.at[rel, k - 1], (lax.rem(grp + k, groups), me))
            copy.start()
            sends.append(copy)

    got[me] = table[me]
    for k in range(cz):
        c = lax.rem(grp + k, cz)
        if k:
            encode(c)
        pencil[me * cz + c] = ecode[c, pl.ds(pl.multiple_of(me * py, py), ext), :]
    count = jnp.where(double, VSLOT, 1)

    def row_of(taps, view):
        rowbuf[...] = jnp.zeros_like(rowbuf)
        rowbuf[0:ranks, 0:width] = taps[view]

    span = rowbuf.shape[1]
    for slot in range(VSLOT):
        view = chosen[slot]
        row_of(kc, view)
        for r in range(ranks):
            t = slot * ranks + r
            line = jnp.broadcast_to(rowbuf[r : r + 1, :], (nx, span))
            band = pltpu.roll(line, span - half, 1, stride=1, stride_axis=0)[:, :nx]
            bx_h[t], bx_l[t] = split(band)
            bxt_h[t], bxt_l[t] = split(band.T)
        row_of(kr, view)
        for r in range(ranks):
            t = slot * ranks + r
            line = jnp.broadcast_to(rowbuf[r : r + 1, 0:128], (py, 128))
            band = pltpu.roll(line, lead - half, 1, stride=1, stride_axis=0)
            byw[t * py : (t + 1) * py, :] = band * weights[slot]
            high, low = split(band[:, :ext] * (1.0 / EST))
            high, low = high.astype(jnp.float32), low.astype(jnp.float32)
            byf[t * py : (t + 1) * py, :] = jnp.concatenate([high * 256.0, high, low * 256.0], axis=1).astype(jnp.bfloat16)
        row_of(kp, view)
        spread8 = lax.broadcasted_iota(jnp.int32, (128, wide), 1) // 8
        spread8 = (spread8 == lax.broadcasted_iota(jnp.int32, (128, wide), 0)).astype(jnp.bfloat16)
        taps = rowbuf[:, 0:128]
        p0 = taps.astype(jnp.bfloat16)
        rest = taps - p0.astype(jnp.float32)
        p1, p2 = split(rest)
        line8 = dot(p0, spread8) + dot(p1, spread8) + dot(p2, spread8)
        line8 = jnp.concatenate([line8, jnp.zeros_like(line8)], axis=1)
        for r in range(ranks):
            t = slot * ranks + r
            line = jnp.broadcast_to(line8[r : r + 1, :], (nz, 2 * wide))
            band = pltpu.roll(line, 2 * wide - 8 * half, 1, stride=8, stride_axis=0)[:, :wide]
            blur[t, 0:nz, :] = band
    turned = byw[...].T[0:ext, 0 : terms * py]
    high, low = split(turned)
    byt[0:ext, :] = high
    byt[ext : 2 * ext, :] = low

    for rel in range(1, blocks):
        src = source(rel)
        remote(table.at[src], got.at[src], sp.at[rel], rp.at[rel], (grp, src)).wait_recv()
    for slot in range(VSLOT):
        for src in range(blocks):
            for j in range(per):
                tile = src * per + j
                pk[8 * tile : 8 * tile + 8, :] = jnp.broadcast_to(got[src, slot * per + j : slot * per + j + 1, :], (8, 128))
        lanes = lax.broadcasted_iota(jnp.int32, (wide, 128), 1)
        hot = (pk[...] == lanes).astype(jnp.float32).astype(jnp.bfloat16)[:, :nz]
        same = (lax.broadcasted_iota(jnp.int32, (wide, wide), 0) % 8) == (lax.broadcasted_iota(jnp.int32, (wide, wide), 1) % 8)
        for r in range(ranks):
            t = slot * ranks + r
            high, low = split(blur[t, 0:nz, :])
            high = jnp.where(same, dot(hot, high), 0.0)
            low = jnp.where(same, dot(hot, low), 0.0)
            kz_h[t] = high.astype(jnp.bfloat16)
            kz_l[t] = low.astype(jnp.bfloat16)
            for value, ref in ((high.T, kzt_h), (low.T, kzt_l)):
                for k in range(blocks):
                    at = ((k % 2) * steps + k // 2) * chunk
                    ref[t, at : at + chunk, :] = value[k * chunk : (k + 1) * chunk].astype(jnp.bfloat16)

    def blur_rows(src):
        for i in range(cz // 2):
            z = src * cz + 2 * i
            pair = []
            for d in range(2):
                code = pencil[z + d].astype(jnp.int32)
                high = ((code >> 8) + 128).astype(jnp.float32).astype(jnp.bfloat16)
                low = (code & 255).astype(jnp.float32).astype(jnp.bfloat16)
                pair.append(dot(byf[...], jnp.concatenate([high, low, high], axis=0)))
            place = pl.ds(pl.multiple_of(z * 8, 16), 16)
            for t in range(terms):
                for y in range(bands8):
                    at = t * py + 8 * y
                    both = jnp.concatenate([pair[0][at : at + 8], pair[1][at : at + 8]], axis=0)
                    high, low = split(both)
                    t1_h[t * bands8 + y, place, :] = high
                    t1_l[t * bands8 + y, place, :] = low

    def blur_cols(rels):
        places = [pl.ds(pl.multiple_of(source(rel) * chunk, chunk), chunk) for rel in rels]

        def cols(t, carry):
            rows = [(t * bands8 + y, place) for y in range(bands8) for place in places]
            value = dot3(
                (
                    jnp.concatenate([t1_h[y, place, :] for y, place in rows], axis=0),
                    jnp.concatenate([t1_l[y, place, :] for y, place in rows], axis=0),
                ),
                (bxt_h[t], bxt_l[t]),
            )
            high, low = split(value)
            for n, (y, place) in enumerate(rows):
                t2_h[y, place, :] = high[n * chunk : (n + 1) * chunk]
                t2_l[y, place, :] = low[n * chunk : (n + 1) * chunk]
            return carry

        lax.fori_loop(0, count * ranks, cols, 0)

    for rel in range(blocks):
        src = source(rel)
        for k in range(1, groups if rel else 1):
            peer = lax.rem(grp + groups - k, groups)
            theirs = pencil.at[src * cz + peer]
            remote(theirs, theirs, sb.at[rel, k - 1], rb.at[rel, k - 1], (peer, me)).wait_recv()
        blur_rows(src)
        if rel == steps - 1:
            blur_cols(range(steps))
    blur_cols(range(steps, blocks))

    def blur_planes(i, carry):
        slot, y = i // bands8, i % bands8
        total = None
        for r in range(ranks):
            t = slot * ranks + r
            piece = dot3((kz_h[t], kz_l[t]), (t2_h[t * bands8 + y], t2_l[t * bands8 + y]))
            total = piece if total is None else total + piece
        blur[i] = total
        return carry

    lax.fori_loop(0, count * bands8, blur_planes, 0)

    def lend(part, src, e):
        return remote(
            arrived.at[part, src, per + e],
            arrived.at[part, src, direct - 1 + grp],
            sq.at[part, src, e], rq.at[part, src, grp - 1], (e * (groups - 1), me),
        )

    @pl.when(jnp.logical_not(double))
    def _():
        a2[ranks * bands8 :] = jnp.zeros(((terms - ranks) * bands8, wide, nx), jnp.float32)

    def take(part):
        for rel in range(blocks):
            src = source(rel)
            if rel > 0:
                here = arrived.at[part, src, pl.ds(0, direct)]
                remote(here, here, st.at[part, rel], rt.at[part, rel], (grp, src)).wait_recv()

                @pl.when(jnp.logical_not(double))
                def _():
                    for e in range(2):
                        lend(part, src, e).start()

                @pl.when(double)
                def _():
                    for w in range(2):
                        there = arrived.at[part, src, direct + w]
                        remote(there, there, sq.at[part, src, w], rq.at[part, src, w], (1 + w, me)).wait_recv()

            for slot in range(VSLOT):
                for j in range(per):
                    tile = arrived[part, src, slot * per + j].astype(jnp.float32)
                    place = pl.ds(pl.multiple_of((src * per + j) * 8, 8), 8)
                    for e in range(2):
                        obs[slot * bands8 + 2 * part + e, place, :] = tile[8 * e : 8 * e + 8]

    for part in range(parts - 1):
        take(part)

        def early(i, carry):
            slot, y = i // 2, 2 * part + i % 2
            ratio = split(obs[slot * bands8 + y] / blur[slot * bands8 + y])
            for r in range(ranks):
                t = slot * ranks + r
                a1 = split(dot3((kzt_h[t], kzt_l[t]), ratio))
                a2[t * bands8 + y] = dot3(a1, (bx_h[t], bx_l[t]))
            return carry

        lax.fori_loop(0, count * 2, early, 0)

    take(parts - 1)
    for slot in range(VSLOT):
        for e in range(2):
            at = slot * bands8 + bands8 - 2 + e
            rat_h[2 * slot + e], rat_l[2 * slot + e] = split(obs[at] / blur[at])

    def halo(k, up):
        rows = pl.ds(k * cz, cz)
        if up:
            return remote(up_s.at[rows], dn_r.at[rows], sh.at[k, 0], rh.at[k, 0], (grp, me - 1))
        return remote(dn_s.at[rows], up_r.at[rows], sh.at[k, 1], rh.at[k, 1], (grp, me + 1))

    span = steps * chunk

    def late(odd):
        place = pl.ds(odd * span, span)

        def one(slot, carry):
            for r in range(ranks):
                t = slot * ranks + r
                both = [
                    dot3((kzt_h[t, place, :], kzt_l[t, place, :]), (rat_h[2 * slot + e], rat_l[2 * slot + e]))
                    for e in range(2)
                ]
                a1 = split(jnp.concatenate(both, axis=0))
                value = dot3(a1, (bx_h[t], bx_l[t]))
                for e in range(2):
                    a2[t * bands8 + bands8 - 2 + e, place, :] = value[e * span : (e + 1) * span]
            return carry

        lax.fori_loop(0, count, one, 0)

    def back(odd):
        def block(n, carry):
            k = 2 * n + odd
            for c in range(cz):
                z = k * cz + c
                at = pl.ds(pl.multiple_of((odd * steps + n) * chunk + 8 * c, 8), 8)
                column = jnp.concatenate([a2[i, at, :] for i in range(terms * bands8)], axis=0)
                high, low = split(column)
                upper = dot(byt[...], high)
                result = upper[:ext] + upper[ext:] + dot(byt[:ext, :], low)
                up_s[z] = halo_code(result[:lead])
                own[z] = result[lead : lead + py]
                dn_s[z] = halo_code(result[lead + py :])

            @pl.when(me > 0)
            def _():
                halo(k, True).start()

            @pl.when(me < blocks - 1)
            def _():
                halo(k, False).start()

            return carry

        lax.fori_loop(0, steps, block, 0)

    first = {}

    def take_halo(odd):
        for n in range(steps):
            k = 2 * n + odd
            rows = pl.ds(k * cz, cz)

            @pl.when(me > 0)
            def _():
                remote(dn_s.at[rows], up_r.at[rows], sh.at[k, 1], rh.at[k, 1], (grp, me - 1)).wait_recv()
                own[rows, 0:lead, :] = own[rows, 0:lead, :] + halo_of(up_r[rows])

            @pl.when(me < blocks - 1)
            def _():
                remote(up_s.at[rows], dn_r.at[rows], sh.at[k, 0], rh.at[k, 0], (grp, me + 1)).wait_recv()
                own[rows, py - lead : py, :] = own[rows, py - lead : py, :] + halo_of(dn_r[rows])

            value = jnp.log(own[rows])
            own[rows] = value
            logs_s[rows] = log_code(value)
            for q in range(1, groups):
                peer = lax.rem(grp + q, groups)
                first[k, q] = remote(
                    logs_s.at[k * cz + peer], logs_r.at[k, q - 1], s1.at[k, q - 1], r1.at[k, q - 1], (peer, me)
                )
                first[k, q].start()

    def mean_out(k):
        return remote(mean_s.at[k], lout.at[grp, strip(me)], s2.at[k], r2.at[me], (grp, k))

    def take_logs(odd):
        for n in range(steps):
            k = 2 * n + odd
            total = own[k * cz + grp]
            for q in range(1, groups):
                first[k, q].wait_recv()
                total = total + log_of(logs_r[k, q - 1])
            mean_s[k] = log_code(total * (1.0 / groups))

            @pl.when(me != k)
            def _():
                mean_out(k).start()

            @pl.when(me == k)
            def _():
                lout[grp, strip(me), :] = mean_s[k]

    def pass_on(src, q):
        here = lout.at[grp, strip(src)]
        return remote(here, here, s3.at[src, q - 1], r3.at[src, q - 1], (lax.rem(grp + q, groups), me))

    def take_mean(odd):
        @pl.when(lax.rem(me, 2) == odd)
        def _():
            for rel in range(blocks):
                src = source(rel)
                here = lout.at[grp, strip(src)]
                if rel > 0:
                    remote(here, here, s2.at[src], r2.at[src], (grp, src)).wait_recv()
                for q in range(1, groups):
                    pass_on(src, q).start()

    late(0)
    back(0)
    late(1)
    take_halo(0)
    back(1)
    take_logs(0)
    take_halo(1)
    take_mean(0)
    take_logs(1)
    take_mean(1)

    for k in range(blocks):
        @pl.when(me > 0)
        def _():
            halo(k, True).wait_send()

        @pl.when(me < blocks - 1)
        def _():
            halo(k, False).wait_send()

        @pl.when(me != k)
        def _():
            mean_out(k).wait_send()

        for q in range(1, groups):
            pass_on(k, q).wait_send()
            first[k, q].wait_send()
    @pl.when(jnp.logical_not(double))
    def _():
        for part in range(parts):
            for rel in range(1, blocks):
                for e in range(2):
                    lend(part, source(rel), e).wait_send()

    for copy in sends:
        copy.wait_send()
    for rel in range(blocks):
        src = source(rel)
        for q in range(1, groups):
            peer = lax.rem(grp + groups - q, groups)
            theirs = lout.at[peer, strip(src)]
            remote(theirs, theirs, s3.at[src, q - 1], r3.at[src, q - 1], (peer, me)).wait_recv()


def fused(estimate, measured, tile_plane, tile_strip, view_group, kernel_cols, kernel_rows, kernel_planes):
    cz, ny, nx = estimate.shape
    blocks = lax.axis_size("blk")
    groups = lax.axis_size("grp")
    nz = cz * blocks
    py = ny // blocks
    ranks, width = kernel_rows.shape[1:]
    lead = -(-(width // 2) // 16) * 16
    ext = py + 2 * lead
    per = measured.shape[1] // blocks
    terms = VSLOT * ranks
    bands8 = py // 8
    parts = py // 16
    wide = 8 * nz
    vmem = pl.BlockSpec(memory_space=pltpu.VMEM)
    smem = pl.BlockSpec(memory_space=pltpu.SMEM)
    anym = pl.BlockSpec(memory_space=pl.ANY)
    dma = pltpu.SemaphoreType.DMA
    f32, b16, i16, i32 = jnp.float32, jnp.bfloat16, jnp.int16, jnp.int32
    square = pltpu.VMEM((terms, nx, nx), b16)
    cube = pltpu.VMEM((terms, wide, wide), b16)
    field = pltpu.VMEM((terms * bands8, wide, nx), b16)
    ratio = pltpu.VMEM((VSLOT * 2, wide, nx), b16)
    edge = pltpu.VMEM((nz, lead, nx), i16)
    batch = pltpu.VMEM((parts, blocks, VSLOT * per, 16, nx), b16)
    listing = pltpu.VMEM((blocks, VSLOT * per, 128), i32)
    lout = pl.pallas_call(
        lambda *refs: fused_kernel(blocks, groups, lead, *refs),
        out_shape=jax.ShapeDtypeStruct((cz, ny, nx), i16),
        in_specs=[smem, smem, smem, anym, anym, vmem, vmem, vmem],
        out_specs=vmem,
        scratch_shapes=[
            pltpu.VMEM(estimate.shape, f32),
            pltpu.VMEM(measured.shape, b16),
            pltpu.VMEM((cz, ny + 2 * lead, nx), i16),
            pltpu.VMEM((nz, ext, nx), i16),
            listing,
            batch, batch,
            listing,
            pltpu.VMEM((8, 2 * nx), f32),
            square, square, square, square,
            cube, cube, cube, cube,
            pltpu.VMEM((terms * py, 3 * ext), b16),
            pltpu.VMEM((2 * ext, terms * py), b16),
            pltpu.VMEM((256, 128), f32),
            pltpu.VMEM((wide, 128), i32),
            field, field, field, field,
            ratio, ratio,
            pltpu.VMEM((VSLOT * bands8, wide, nx), f32),
            pltpu.VMEM((VSLOT * bands8, wide, nx), f32),
            pltpu.VMEM((terms * bands8, wide, nx), f32),
            pltpu.VMEM((nz, py, nx), f32),
            edge, edge, edge, edge,
            pltpu.VMEM((nz, py, nx), i16),
            pltpu.VMEM((blocks, groups - 1, py, nx), i16),
            pltpu.VMEM((blocks, py, nx), i16),
            dma((2,)),
            dma((blocks,)), dma((blocks,)),
            dma((blocks, groups - 1)), dma((blocks, groups - 1)),
            dma((blocks,)), dma((blocks,)),
            dma((parts, blocks)), dma((parts, blocks)),
            dma((parts, blocks, 2)), dma((parts, blocks, 2)),
            dma((blocks, 2)), dma((blocks, 2)),
            dma((blocks, groups - 1)), dma((blocks, groups - 1)),
            dma((blocks,)), dma((blocks,)),
            dma((blocks, groups - 1)), dma((blocks, groups - 1)),
        ],
        compiler_params=pltpu.CompilerParams(collective_id=2, has_side_effects=True, vmem_limit_bytes=60 * 2**20),
        name="fused",
    )(view_group, tile_plane, tile_strip, estimate, measured, kernel_cols, kernel_rows, kernel_planes)
    return estimate * jnp.exp(log_of(lout))


def shards(estimate, measured, tile_plane, tile_strip, view_group, kernel_cols, kernel_rows, kernel_planes):
    cz, ny, nx = estimate.shape
    blocks = lax.axis_size("blk")
    groups = lax.axis_size("grp")
    py = ny // blocks
    half = kernel_rows.shape[-1] // 2
    lead = -(-half // 16) * 16
    per = measured.shape[1] // blocks
    fits = (
        cz == groups
        and cz % 2 == 0
        and blocks % 2 == 0
        and py % 16 == 0
        and py >= lead
        and py + 2 * lead <= 128
        and measured.shape[2] == py
        and nx % 128 == 0
        and VSLOT * per == 8
        and groups == 4
        and view_group.shape[0] == groups + 2
        and VSLOT * kernel_rows.shape[1] * py <= 256
        and per * (measured.shape[1] - 1).bit_length() <= 31
        and (8 * cz * blocks) % 128 == 0
        and cz * blocks <= 64
    )
    program = fused if fits else general
    return program(estimate, measured, tile_plane, tile_strip, view_group, kernel_cols, kernel_rows, kernel_planes)


def solution(mesh):
    in_specs = (
        P("blk", None, None),
        P(None, "blk", None, None),
        P(None, "blk"),
        P(None, "blk"),
        P(),
        P(),
        P(),
        P(),
    )
    return jax.shard_map(
        shards, mesh=mesh, in_specs=in_specs, out_specs=P("blk", None, None), check_vma=False
    )
```

```python
import jax
import jax.numpy as jnp
from jax import lax
from jax.experimental import pallas as pl
from jax.experimental.pallas import tpu as pltpu
from jax.sharding import PartitionSpec as P

VSLOT = 2
HIGH = lax.Precision.HIGH


MESH = pl.DeviceIdType.MESH


def band_kernel(*refs):
    count = len(refs) // 2
    for row, out in zip(refs[:count], refs[count:]):
        number, rows, cols = out.shape
        for n in range(number):
            wide = jnp.broadcast_to(row[n], (rows, row.shape[-1]))
            wide = pltpu.roll(wide, 0, 1, stride=1, stride_axis=0)
            out[n] = wide[:, :cols]


def bands(shapes):
    rows_in, outs = [], []
    for taps, rows, cols, lead in shapes:
        number, width = taps.shape
        half = width // 2
        span = -(-(max(cols, rows) + lead + width) // 128) * 128
        row = jnp.pad(taps, ((0, 0), (0, span - width)))
        row = jnp.roll(row, lead - half, axis=1)
        rows_in.append(row[:, None, :])
        outs.append(jax.ShapeDtypeStruct((number, rows, cols), jnp.float32))
    vmem = pl.BlockSpec(memory_space=pltpu.VMEM)
    return pl.pallas_call(
        band_kernel,
        out_shape=outs,
        in_specs=[vmem] * len(outs),
        out_specs=[vmem] * len(outs),
    )(*rows_in)


def spread_kernel(blocks, groups, step, padded, planes, tiles, pencil, got, arrived, sa, ra, sb, rb, sp, rp, st, rt):
    me = lax.axis_index("blk")
    grp = lax.axis_index("grp")
    cz, span = pencil.shape[1], pencil.shape[2]
    cq = cz // groups
    mine = pl.ds(grp * cq, cq)
    barrier = pltpu.get_barrier_semaphore()
    for k in range(1, groups):
        pl.semaphore_signal(barrier, inc=1, device_id=(lax.rem(grp + k, groups), me), device_id_type=MESH)
    for rel in range(1, blocks):
        pl.semaphore_signal(barrier, inc=1, device_id=(grp, lax.rem(me + rel, blocks)), device_id_type=MESH)
    pl.semaphore_wait(barrier, groups + blocks - 2)

    first, small, second, large = {}, {}, {}, {}
    for rel in range(1, blocks):
        dest = lax.rem(me + rel, blocks)
        first[rel] = pltpu.make_async_remote_copy(
            src_ref=padded.at[mine, pl.ds(dest * step, span)],
            dst_ref=pencil.at[me, mine],
            send_sem=sa.at[rel],
            recv_sem=ra.at[rel],
            device_id=(grp, dest),
            device_id_type=MESH,
        )
        first[rel].start()
    for rel in range(1, blocks):
        dest = lax.rem(me + rel, blocks)
        small[rel] = pltpu.make_async_remote_copy(
            src_ref=planes.at[dest],
            dst_ref=got.at[me],
            send_sem=sp.at[rel],
            recv_sem=rp.at[rel],
            device_id=(grp, dest),
            device_id_type=MESH,
        )
        small[rel].start()
    for rel in range(1, blocks):
        dest = lax.rem(me + rel, blocks)
        large[rel] = pltpu.make_async_remote_copy(
            src_ref=tiles.at[dest],
            dst_ref=arrived.at[me],
            send_sem=st.at[rel],
            recv_sem=rt.at[rel],
            device_id=(grp, dest),
            device_id_type=MESH,
        )
        large[rel].start()
    arrived[me] = tiles[me]
    pencil[me] = padded[:, pl.ds(me * step, span)]
    got[me] = planes[me]
    for rel in range(1, blocks):
        src = lax.rem(me + blocks - rel, blocks)
        landed = pencil.at[src, mine]
        pltpu.make_async_remote_copy(
            src_ref=landed,
            dst_ref=landed,
            send_sem=sa.at[rel],
            recv_sem=ra.at[rel],
            device_id=(grp, src),
            device_id_type=MESH,
        ).wait_recv()
        for k in range(1, groups):
            second[rel, k] = pltpu.make_async_remote_copy(
                src_ref=landed,
                dst_ref=landed,
                send_sem=sb.at[rel, k - 1],
                recv_sem=rb.at[rel, k - 1],
                device_id=(lax.rem(grp + k, groups), me),
                device_id_type=MESH,
            )
            second[rel, k].start()
    for rel in range(1, blocks):
        src = lax.rem(me + blocks - rel, blocks)
        for k in range(1, groups):
            peer = lax.rem(grp + groups - k, groups)
            theirs = pencil.at[src, pl.ds(peer * cq, cq)]
            pltpu.make_async_remote_copy(
                src_ref=theirs,
                dst_ref=theirs,
                send_sem=sb.at[rel, k - 1],
                recv_sem=rb.at[rel, k - 1],
                device_id=(peer, me),
                device_id_type=MESH,
            ).wait_recv()
        pltpu.make_async_remote_copy(
            src_ref=planes.at[src],
            dst_ref=got.at[src],
            send_sem=sp.at[rel],
            recv_sem=rp.at[rel],
            device_id=(grp, src),
            device_id_type=MESH,
        ).wait_recv()
        pltpu.make_async_remote_copy(
            src_ref=tiles.at[src],
            dst_ref=arrived.at[src],
            send_sem=st.at[rel],
            recv_sem=rt.at[rel],
            device_id=(grp, src),
            device_id_type=MESH,
        ).wait_recv()
    for copies in (first, small, second, large):
        for copy in copies.values():
            copy.wait_send()


def spread(estimate, planes, tiles, lead, blocks, groups):
    cz, ny, nx = estimate.shape
    py = ny // blocks
    chunk = min(py, lead)
    span = (py + 2 * lead) // chunk
    padded = jnp.pad(estimate, ((0, 0), (lead, lead), (0, 0))).reshape(cz, -1, chunk, nx)
    vmem = pl.BlockSpec(memory_space=pltpu.VMEM)
    dma = pltpu.SemaphoreType.DMA
    pencil, got, arrived = pl.pallas_call(
        lambda *refs: spread_kernel(blocks, groups, py // chunk, *refs),
        out_shape=[
            jax.ShapeDtypeStruct((blocks, cz, span, chunk, nx), jnp.float32),
            jax.ShapeDtypeStruct(planes.shape, jnp.int32),
            jax.ShapeDtypeStruct(tiles.shape, tiles.dtype),
        ],
        in_specs=[vmem] * 3,
        out_specs=[vmem] * 3,
        scratch_shapes=[
            dma((blocks,)),
            dma((blocks,)),
            dma((blocks, groups - 1)),
            dma((blocks, groups - 1)),
            dma((blocks,)),
            dma((blocks,)),
            dma((blocks,)),
            dma((blocks,)),
        ],
        compiler_params=pltpu.CompilerParams(collective_id=1, has_side_effects=True),
        cost_estimate=pl.CostEstimate(flops=0, bytes_accessed=1 << 26, transcendentals=0),
        name="spread",
    )(padded, planes, tiles)
    return pencil.reshape(cz * blocks, py + 2 * lead, nx), got, arrived


def finish_kernel(blocks, groups, logs, est, out, got1, send2, got2, s1, r1, s2, r2, s3, r3):
    me = lax.axis_index("blk")
    grp = lax.axis_index("grp")
    cq = est.shape[0] // groups
    mine = pl.ds(grp * cq, cq)
    barrier = pltpu.get_barrier_semaphore()
    for k in range(1, groups):
        pl.semaphore_signal(barrier, inc=1, device_id=(lax.rem(grp + k, groups), me), device_id_type=MESH)
    for rel in range(1, blocks):
        pl.semaphore_signal(barrier, inc=1, device_id=(grp, lax.rem(me + rel, blocks)), device_id_type=MESH)
    pl.semaphore_wait(barrier, groups + blocks - 2)
    order = list(range(1, blocks)) + [0]

    first, second, third = {}, {}, {}
    for rel in order:
        dest = lax.rem(me + rel, blocks)
        for k in range(1, groups):
            peer = lax.rem(grp + k, groups)
            first[rel, k] = pltpu.make_async_remote_copy(
                src_ref=logs.at[dest, pl.ds(peer * cq, cq)],
                dst_ref=got1.at[rel, k - 1],
                send_sem=s1.at[rel, k - 1],
                recv_sem=r1.at[rel, k - 1],
                device_id=(peer, me),
                device_id_type=MESH,
            )
            first[rel, k].start()
    for rel in order:
        dest = lax.rem(me + rel, blocks)
        total = logs[dest, mine]
        for k in range(1, groups):
            first[rel, k].wait_recv()
            total = total + got1[rel, k - 1]
        if rel == 0:
            got2[0] = total
        else:
            send2[rel] = total
            second[rel] = pltpu.make_async_remote_copy(
                src_ref=send2.at[rel],
                dst_ref=got2.at[rel],
                send_sem=s2.at[rel],
                recv_sem=r2.at[rel],
                device_id=(grp, dest),
                device_id_type=MESH,
            )
            second[rel].start()
    for rel in order:
        strip = lax.rem(me + blocks - rel, blocks)
        if rel != 0:
            second[rel].wait_recv()
        out[mine, strip] = est[mine, strip] * jnp.exp(got2[rel] * (1.0 / groups))
        for k in range(1, groups):
            third[rel, k] = pltpu.make_async_remote_copy(
                src_ref=out.at[mine, strip],
                dst_ref=out.at[mine, strip],
                send_sem=s3.at[rel, k - 1],
                recv_sem=r3.at[rel, k - 1],
                device_id=(lax.rem(grp + k, groups), me),
                device_id_type=MESH,
            )
            third[rel, k].start()
    for copy in first.values():
        copy.wait_send()
    for copy in second.values():
        copy.wait_send()
    for copy in third.values():
        copy.wait_send()
    for rel in order:
        strip = lax.rem(me + blocks - rel, blocks)
        for k in range(1, groups):
            peer = lax.rem(grp + groups - k, groups)
            theirs = out.at[pl.ds(peer * cq, cq), strip]
            pltpu.make_async_remote_copy(
                src_ref=theirs,
                dst_ref=theirs,
                send_sem=s3.at[rel, k - 1],
                recv_sem=r3.at[rel, k - 1],
                device_id=(peer, me),
                device_id_type=MESH,
            ).wait_recv()


def finish(logs, estimate, blocks, groups):
    cz, ny, nx = estimate.shape
    py = ny // blocks
    cq = cz // groups
    vmem = pl.BlockSpec(memory_space=pltpu.VMEM)
    dma = pltpu.SemaphoreType.DMA
    out = pl.pallas_call(
        lambda *refs: finish_kernel(blocks, groups, *refs),
        out_shape=jax.ShapeDtypeStruct((cz, blocks, py, nx), jnp.float32),
        in_specs=[vmem, vmem],
        out_specs=vmem,
        scratch_shapes=[
            pltpu.VMEM((blocks, groups - 1, cq, py, nx), jnp.float32),
            pltpu.VMEM((blocks, cq, py, nx), jnp.float32),
            pltpu.VMEM((blocks, cq, py, nx), jnp.float32),
            dma((blocks, groups - 1)),
            dma((blocks, groups - 1)),
            dma((blocks,)),
            dma((blocks,)),
            dma((blocks, groups - 1)),
            dma((blocks, groups - 1)),
        ],
        compiler_params=pltpu.CompilerParams(collective_id=0, has_side_effects=True),
        name="finish",
    )(logs.reshape(blocks, cz, py, nx), estimate.reshape(cz, blocks, py, nx))
    return out.reshape(cz, ny, nx)


def general(estimate, measured, tile_plane, tile_strip, view_group, kernel_cols, kernel_rows, kernel_planes):
    cz, ny, nx = estimate.shape
    blocks = lax.axis_size("blk")
    groups = lax.axis_size("grp")
    nz = cz * blocks
    py = ny // blocks
    half = kernel_rows.shape[-1] // 2
    lead = -(-half // 8) * 8
    ext = py + 2 * lead
    tiles = measured.shape[1]
    per = tiles // blocks

    matches = (view_group == lax.axis_index("grp")).astype(jnp.int32)
    members = jnp.sum(matches).astype(jnp.float32)
    ids = jnp.arange(view_group.shape[0], dtype=jnp.int32)
    ranking = jnp.sum(jnp.where(ids[None, :] < ids[:, None], matches[None, :], 0), axis=1)
    picked = [matches * (ranking == s).astype(jnp.int32) for s in range(VSLOT)]
    chosen = [jnp.sum(p * ids) for p in picked]
    weights = jnp.stack([jnp.sum(p).astype(jnp.float32) / members for p in picked])

    pick = lambda a: jnp.stack([lax.dynamic_index_in_dim(a, c, 0, keepdims=False) for c in chosen])
    pieces, planes, strips = pick(measured), pick(tile_plane), pick(tile_strip)
    number = jnp.arange(tiles, dtype=jnp.int32)
    earlier = (strips[:, :, None] == strips[:, None, :]) & (number[None, :] < number[:, None])
    positions = strips * per + jnp.sum(earlier.astype(jnp.int32), axis=2)
    order = positions[:, None, :] == jnp.arange(tiles, dtype=jnp.int32)[None, :, None]
    send_planes = jnp.sum(jnp.where(order, planes[:, None, :], 0), axis=2)
    send = jnp.einsum("vpi,viyx->pvyx", order.astype(jnp.bfloat16), pieces)
    send = send.reshape(blocks, per, VSLOT, py, nx)

    table = send_planes.reshape(VSLOT, blocks, per).transpose(1, 0, 2)
    table = jnp.pad(table, ((0, 0), (0, 8 - VSLOT), (0, 128 - per)))
    pencil, table, got = spread(estimate, table, send, lead, blocks, groups)
    got = got.reshape(tiles, VSLOT, py, nx)
    got_planes = table[:, :VSLOT, :per].transpose(0, 2, 1).reshape(tiles, VSLOT)
    place = (got_planes[None] == jnp.arange(nz, dtype=jnp.int32)[:, None, None]).astype(jnp.bfloat16)
    observed = jnp.einsum("ptv,tvyx->vpyx", place, got).astype(jnp.float32)

    kc, kr, kp = pick(kernel_cols), pick(kernel_rows), pick(kernel_planes)
    flat = lambda k: k.reshape(-1, k.shape[-1])
    fold = lambda m: m.reshape((VSLOT, -1) + m.shape[1:])
    bx, by, bz = map(fold, bands([(flat(kc), nx, nx, 0), (flat(kr), py, ext, lead), (flat(kp), nz, nz, 0)]))
    byw = by * weights[:, None, None, None]

    t = jnp.einsum("zmx,vrim->vrzix", pencil, by, precision=HIGH)
    t = jnp.einsum("vrzix,vrnx->vrzin", t, bx, precision=HIGH)
    blurred = jnp.einsum("vrzin,vrpz->vpin", t, bz, precision=HIGH)
    ratios = observed / blurred
    a = jnp.einsum("vpin,vrpz->vrzin", ratios, bz, precision=HIGH)
    a = jnp.einsum("vrzin,vrnx->vrzix", a, bx, precision=HIGH)
    wide = jnp.einsum("vrzix,vrim->zmx", a, byw, precision=HIGH)

    chunk = min(py, lead)
    average = wide[:, lead : lead + py]
    for d in range(1, lead // chunk + 1):
        up = wide[:, lead + py + (d - 1) * chunk : lead + py + d * chunk]
        down = wide[:, lead - d * chunk : lead - (d - 1) * chunk]
        up = lax.ppermute(up, "blk", [(i, i + d) for i in range(blocks - d)])
        down = lax.ppermute(down, "blk", [(i, i - d) for i in range(d, blocks)])
        rest = py - chunk
        average = average + jnp.pad(up, ((0, 0), (0, rest), (0, 0))) + jnp.pad(down, ((0, 0), (rest, 0), (0, 0)))
    logs = jnp.log(average)
    return finish(logs, estimate, blocks, groups)


def split(value):
    high = value.astype(jnp.bfloat16)
    low = (value - high.astype(jnp.float32)).astype(jnp.bfloat16)
    return high, low


def dot(a, b):
    return jnp.dot(a, b, preferred_element_type=jnp.float32)


def dot3(a, b):
    return dot(jnp.concatenate([a[0], a[1], a[0]], axis=1), jnp.concatenate([b[0], b[0], b[1]], axis=0))


EST = 16383.0
HALO = 65534.0
LOG = 32767.0
KNEE = 4.0


def to_code(value):
    return ((value + 0.5).astype(jnp.int32) - 32768).astype(jnp.int16)


def log_code(logs):
    return to_code(logs / (KNEE + jnp.abs(logs)) * LOG + 32768.0)


def log_of(code):
    value = code.astype(jnp.int32).astype(jnp.float32) * (1.0 / LOG)
    return KNEE * value / (1.0 - jnp.abs(value))


def halo_code(value):
    return to_code(value / (1.0 + value) * HALO)


def halo_of(code):
    value = (code.astype(jnp.int32) + 32768).astype(jnp.float32) * (1.0 / HALO)
    return value / (1.0 - value)


def fused_kernel(
    blocks, groups, lead,
    view_group, tile_plane, tile_strip, estimate, measured, kc, kr, kp,
    lout,
    est, stage, ecode, pencil, table, sendt, arrived, got, rowbuf,
    bxt_h, bxt_l, bx_h, bx_l, kz_h, kz_l, kzt_h, kzt_l, byf, byt, byw, pk,
    t1_h, t1_l, t2_h, t2_l, rat_h, rat_l, blur, obs, a2, own, up_s, dn_s, up_r, dn_r, logs_s, logs_r, mean_s,
    sm, sa, ra, sb, rb, sp, rp, st, rt, sq, rq, sh, rh, s1, r1, s2, r2, s3, r3,
):
    me = lax.axis_index("blk")
    grp = lax.axis_index("grp")
    cz, ny, nx = est.shape
    views, tiles = tile_plane.shape
    py = ny // blocks
    nz = cz * blocks
    ext = py + 2 * lead
    ranks, width = kc.shape[1], kc.shape[2]
    half = width // 2
    terms = VSLOT * ranks
    per = tiles // blocks
    bands8 = py // 8
    parts = py // 16
    wide = 8 * nz
    chunk = 8 * cz
    steps = blocks // 2

    def remote(src, dst, send, recv, to):
        return pltpu.make_async_remote_copy(
            src_ref=src, dst_ref=dst, send_sem=send, recv_sem=recv, device_id=to, device_id_type=MESH
        )

    def source(rel):
        return lax.rem(me + blocks - rel, blocks)

    def strip(index):
        return pl.ds(pl.multiple_of(index * py, py), py)

    double = (grp == 0) | (grp == groups - 1)
    direct = per + per // 2
    fetch = pltpu.make_async_copy(estimate, est, sm.at[0])
    fetch.start()
    load = pltpu.make_async_copy(measured, stage, sm.at[1])
    load.start()
    for part in range(parts):
        arrived[part, :, direct:] = jnp.zeros((blocks, VSLOT * per - direct, 16, nx), jnp.bfloat16)
    barrier = pltpu.get_barrier_semaphore()
    for k in range(1, groups):
        pl.semaphore_signal(barrier, inc=1, device_id=(lax.rem(grp + k, groups), me), device_id_type=MESH)
    for rel in range(1, blocks):
        pl.semaphore_signal(barrier, inc=1, device_id=(grp, lax.rem(me + rel, blocks)), device_id_type=MESH)

    def encode(c):
        ecode[c, 0:lead, :] = jnp.full((lead, nx), -32768, jnp.int16)
        ecode[c, lead + ny : lead + ny + lead, :] = jnp.full((lead, nx), -32768, jnp.int16)
        ecode[c, lead : lead + ny, :] = to_code(est[c] * EST)

    fetch.wait()
    encode(grp)
    pl.semaphore_wait(barrier, groups + blocks - 2)

    sends = []
    for rel in range(1, blocks):
        dest = lax.rem(me + rel, blocks)
        copy = remote(
            ecode.at[grp, pl.ds(pl.multiple_of(dest * py, py), ext)],
            pencil.at[me * cz + grp],
            sa.at[rel], ra.at[rel], (grp, dest),
        )
        copy.start()
        sends.append(copy)

    holds = [jnp.int32(0)] * groups
    doubles, singles = jnp.int32(0), jnp.int32(0)
    for group in range(groups):
        size = jnp.int32(0)
        for view in range(views):
            size = size + (view_group[view] == group).astype(jnp.int32)
        two = size > 1
        column = jnp.where(two, doubles * (groups - 1), 1 + singles)
        doubles = doubles + two.astype(jnp.int32)
        singles = singles + 1 - two.astype(jnp.int32)
        holds = [jnp.where(column == c, group, h) for c, h in enumerate(holds)]
    mine = holds[0]
    for c in range(1, groups):
        mine = jnp.where(grp == c, holds[c], mine)

    def views_of(group):
        low, high = jnp.int32(views), jnp.int32(0)
        for view in range(views):
            match = view_group[view] == group
            low = jnp.where(match, jnp.minimum(low, view), low)
            high = jnp.where(match, view, high)
        return jnp.minimum(low, views - 1), high

    own_views = views_of(mine)
    ends = (views_of(holds[0])[1], views_of(holds[groups - 1])[1])
    chosen = own_views
    listed = (own_views[0], jnp.where(double, own_views[1], ends[0]), jnp.where(double, own_views[1], ends[1]))
    weights = (jnp.where(double, 1.0 / VSLOT, 1.0), jnp.where(double, 1.0 / VSLOT, 0.0))
    bits = (tiles - 1).bit_length()
    order = []
    for slot in range(len(listed)):
        packed = [jnp.int32(0)] * blocks
        for tile in range(tiles):
            where = tile_strip[listed[slot], tile]
            packed = [jnp.where(where == d, (p << bits) + tile, p) for d, p in enumerate(packed)]
        order.append([[(p >> (bits * j)) & ((1 << bits) - 1) for j in range(per)] for p in packed])
    for d in range(blocks):
        for slot in range(VSLOT):
            for j in range(per):
                plane = tile_plane[listed[slot], order[slot][d][j]]
                table[d, slot * per + j : slot * per + j + 1, :] = jnp.full((1, 128), plane, jnp.int32)
    for rel in range(1, blocks):
        dest = lax.rem(me + rel, blocks)
        copy = remote(table.at[dest], got.at[me], sp.at[rel], rp.at[rel], (grp, dest))
        copy.start()
        sends.append(copy)
    load.wait()
    for part in range(parts):
        for d in range(blocks):
            picks = [(listed[0], order[0][d][j]) for j in range(per)]
            for e in range(per // 2):
                one = order[1 + e][d]
                lent = jnp.where(grp == 1, one[per // 2], one[per // 2 + 1])
                picks.append((listed[1 + e], jnp.where(double, one[e], lent)))
            picks += [(listed[1], order[1][d][j]) for j in range(per // 2, per)]
            for e, (view, tile) in enumerate(picks):
                sendt[part, d, e] = stage[view, tile, 16 * part : 16 * part + 16, :]
        for rel in range(1, blocks):
            dest = lax.rem(me + rel, blocks)
            copy = remote(
                sendt.at[part, dest, pl.ds(0, direct)],
                arrived.at[part, me, pl.ds(0, direct)],
                st.at[part, rel], rt.at[part, rel], (grp, dest),
            )
            copy.start()
            sends.append(copy)
        arrived[part, me] = sendt[part, me]
    for rel in range(1, blocks):
        src = source(rel)
        landed = pencil.at[src * cz + grp]
        remote(landed, landed, sa.at[rel], ra.at[rel], (grp, src)).wait_recv()
        for k in range(1, groups):
            copy = remote(landed, landed, sb.at[rel, k - 1], rb.at[rel, k - 1], (lax.rem(grp + k, groups), me))
            copy.start()
            sends.append(copy)

    got[me] = table[me]
    for k in range(cz):
        c = lax.rem(grp + k, cz)
        if k:
            encode(c)
        pencil[me * cz + c] = ecode[c, pl.ds(pl.multiple_of(me * py, py), ext), :]
    count = jnp.where(double, VSLOT, 1)

    def row_of(taps, view):
        rowbuf[...] = jnp.zeros_like(rowbuf)
        rowbuf[0:ranks, 0:width] = taps[view]

    span = rowbuf.shape[1]
    for slot in range(VSLOT):
        view = chosen[slot]
        row_of(kc, view)
        for r in range(ranks):
            t = slot * ranks + r
            line = jnp.broadcast_to(rowbuf[r : r + 1, :], (nx, span))
            band = pltpu.roll(line, span - half, 1, stride=1, stride_axis=0)[:, :nx]
            bx_h[t], bx_l[t] = split(band)
            bxt_h[t], bxt_l[t] = split(band.T)
        row_of(kr, view)
        for r in range(ranks):
            t = slot * ranks + r
            line = jnp.broadcast_to(rowbuf[r : r + 1, 0:128], (py, 128))
            band = pltpu.roll(line, lead - half, 1, stride=1, stride_axis=0)
            byw[t * py : (t + 1) * py, :] = band * weights[slot]
            high, low = split(band[:, :ext] * (1.0 / EST))
            high, low = high.astype(jnp.float32), low.astype(jnp.float32)
            byf[t * py : (t + 1) * py, :] = jnp.concatenate([high * 256.0, high, low * 256.0], axis=1).astype(jnp.bfloat16)
        row_of(kp, view)
        spread8 = lax.broadcasted_iota(jnp.int32, (128, wide), 1) // 8
        spread8 = (spread8 == lax.broadcasted_iota(jnp.int32, (128, wide), 0)).astype(jnp.bfloat16)
        taps = rowbuf[:, 0:128]
        p0 = taps.astype(jnp.bfloat16)
        rest = taps - p0.astype(jnp.float32)
        p1, p2 = split(rest)
        line8 = dot(p0, spread8) + dot(p1, spread8) + dot(p2, spread8)
        line8 = jnp.concatenate([line8, jnp.zeros_like(line8)], axis=1)
        for r in range(ranks):
            t = slot * ranks + r
            line = jnp.broadcast_to(line8[r : r + 1, :], (nz, 2 * wide))
            band = pltpu.roll(line, 2 * wide - 8 * half, 1, stride=8, stride_axis=0)[:, :wide]
            blur[t, 0:nz, :] = band
    turned = byw[...].T[0:ext, 0 : terms * py]
    high, low = split(turned)
    byt[0:ext, :] = high
    byt[ext : 2 * ext, :] = low

    for rel in range(1, blocks):
        src = source(rel)
        remote(table.at[src], got.at[src], sp.at[rel], rp.at[rel], (grp, src)).wait_recv()
    for slot in range(VSLOT):
        for src in range(blocks):
            for j in range(per):
                tile = src * per + j
                pk[8 * tile : 8 * tile + 8, :] = jnp.broadcast_to(got[src, slot * per + j : slot * per + j + 1, :], (8, 128))
        lanes = lax.broadcasted_iota(jnp.int32, (wide, 128), 1)
        hot = (pk[...] == lanes).astype(jnp.float32).astype(jnp.bfloat16)[:, :nz]
        same = (lax.broadcasted_iota(jnp.int32, (wide, wide), 0) % 8) == (lax.broadcasted_iota(jnp.int32, (wide, wide), 1) % 8)
        for r in range(ranks):
            t = slot * ranks + r
            high, low = split(blur[t, 0:nz, :])
            high = jnp.where(same, dot(hot, high), 0.0)
            low = jnp.where(same, dot(hot, low), 0.0)
            kz_h[t] = high.astype(jnp.bfloat16)
            kz_l[t] = low.astype(jnp.bfloat16)
            for value, ref in ((high.T, kzt_h), (low.T, kzt_l)):
                for k in range(blocks):
                    at = ((k % 2) * steps + k // 2) * chunk
                    ref[t, at : at + chunk, :] = value[k * chunk : (k + 1) * chunk].astype(jnp.bfloat16)

    def blur_rows(src):
        for i in range(cz // 2):
            z = src * cz + 2 * i
            pair = []
            for d in range(2):
                code = pencil[z + d].astype(jnp.int32)
                high = ((code >> 8) + 128).astype(jnp.float32).astype(jnp.bfloat16)
                low = (code & 255).astype(jnp.float32).astype(jnp.bfloat16)
                pair.append(dot(byf[...], jnp.concatenate([high, low, high], axis=0)))
            place = pl.ds(pl.multiple_of(z * 8, 16), 16)
            for t in range(terms):
                for y in range(bands8):
                    at = t * py + 8 * y
                    both = jnp.concatenate([pair[0][at : at + 8], pair[1][at : at + 8]], axis=0)
                    high, low = split(both)
                    t1_h[t * bands8 + y, place, :] = high
                    t1_l[t * bands8 + y, place, :] = low

    def blur_cols(rels):
        places = [pl.ds(pl.multiple_of(source(rel) * chunk, chunk), chunk) for rel in rels]

        def cols(t, carry):
            rows = [(t * bands8 + y, place) for y in range(bands8) for place in places]
            value = dot3(
                (
                    jnp.concatenate([t1_h[y, place, :] for y, place in rows], axis=0),
                    jnp.concatenate([t1_l[y, place, :] for y, place in rows], axis=0),
                ),
                (bxt_h[t], bxt_l[t]),
            )
            high, low = split(value)
            for n, (y, place) in enumerate(rows):
                t2_h[y, place, :] = high[n * chunk : (n + 1) * chunk]
                t2_l[y, place, :] = low[n * chunk : (n + 1) * chunk]
            return carry

        lax.fori_loop(0, count * ranks, cols, 0)

    for rel in range(blocks):
        src = source(rel)
        for k in range(1, groups if rel else 1):
            peer = lax.rem(grp + groups - k, groups)
            theirs = pencil.at[src * cz + peer]
            remote(theirs, theirs, sb.at[rel, k - 1], rb.at[rel, k - 1], (peer, me)).wait_recv()
        blur_rows(src)
        if rel == steps - 1:
            blur_cols(range(steps))
    blur_cols(range(steps, blocks))

    def blur_planes(i, carry):
        slot, y = i // bands8, i % bands8
        total = None
        for r in range(ranks):
            t = slot * ranks + r
            piece = dot3((kz_h[t], kz_l[t]), (t2_h[t * bands8 + y], t2_l[t * bands8 + y]))
            total = piece if total is None else total + piece
        blur[i] = total
        return carry

    lax.fori_loop(0, count * bands8, blur_planes, 0)

    def lend(part, src, e):
        return remote(
            arrived.at[part, src, per + e],
            arrived.at[part, src, direct - 1 + grp],
            sq.at[part, src, e], rq.at[part, src, grp - 1], (e * (groups - 1), me),
        )

    @pl.when(jnp.logical_not(double))
    def _():
        a2[ranks * bands8 :] = jnp.zeros(((terms - ranks) * bands8, wide, nx), jnp.float32)

    def take(part):
        for rel in range(blocks):
            src = source(rel)
            if rel > 0:
                here = arrived.at[part, src, pl.ds(0, direct)]
                remote(here, here, st.at[part, rel], rt.at[part, rel], (grp, src)).wait_recv()

                @pl.when(jnp.logical_not(double))
                def _():
                    for e in range(2):
                        lend(part, src, e).start()

                @pl.when(double)
                def _():
                    for w in range(2):
                        there = arrived.at[part, src, direct + w]
                        remote(there, there, sq.at[part, src, w], rq.at[part, src, w], (1 + w, me)).wait_recv()

            for slot in range(VSLOT):
                for j in range(per):
                    tile = arrived[part, src, slot * per + j].astype(jnp.float32)
                    place = pl.ds(pl.multiple_of((src * per + j) * 8, 8), 8)
                    for e in range(2):
                        obs[slot * bands8 + 2 * part + e, place, :] = tile[8 * e : 8 * e + 8]

    for part in range(parts - 1):
        take(part)

        def early(i, carry):
            slot, y = i // 2, 2 * part + i % 2
            ratio = split(obs[slot * bands8 + y] / blur[slot * bands8 + y])
            for r in range(ranks):
                t = slot * ranks + r
                a1 = split(dot3((kzt_h[t], kzt_l[t]), ratio))
                a2[t * bands8 + y] = dot3(a1, (bx_h[t], bx_l[t]))
            return carry

        lax.fori_loop(0, count * 2, early, 0)

    take(parts - 1)
    for slot in range(VSLOT):
        for e in range(2):
            at = slot * bands8 + bands8 - 2 + e
            rat_h[2 * slot + e], rat_l[2 * slot + e] = split(obs[at] / blur[at])

    def halo(k, up):
        rows = pl.ds(k * cz, cz)
        if up:
            return remote(up_s.at[rows], dn_r.at[rows], sh.at[k, 0], rh.at[k, 0], (grp, me - 1))
        return remote(dn_s.at[rows], up_r.at[rows], sh.at[k, 1], rh.at[k, 1], (grp, me + 1))

    span = steps * chunk

    def late(odd):
        place = pl.ds(odd * span, span)

        def one(slot, carry):
            for r in range(ranks):
                t = slot * ranks + r
                both = [
                    dot3((kzt_h[t, place, :], kzt_l[t, place, :]), (rat_h[2 * slot + e], rat_l[2 * slot + e]))
                    for e in range(2)
                ]
                a1 = split(jnp.concatenate(both, axis=0))
                value = dot3(a1, (bx_h[t], bx_l[t]))
                for e in range(2):
                    a2[t * bands8 + bands8 - 2 + e, place, :] = value[e * span : (e + 1) * span]
            return carry

        lax.fori_loop(0, count, one, 0)

    def back(odd):
        def block(n, carry):
            k = 2 * n + odd
            for c in range(cz):
                z = k * cz + c
                at = pl.ds(pl.multiple_of((odd * steps + n) * chunk + 8 * c, 8), 8)
                column = jnp.concatenate([a2[i, at, :] for i in range(terms * bands8)], axis=0)
                high, low = split(column)
                upper = dot(byt[...], high)
                result = upper[:ext] + upper[ext:] + dot(byt[:ext, :], low)
                up_s[z] = halo_code(result[:lead])
                own[z] = result[lead : lead + py]
                dn_s[z] = halo_code(result[lead + py :])

            @pl.when(me > 0)
            def _():
                halo(k, True).start()

            @pl.when(me < blocks - 1)
            def _():
                halo(k, False).start()

            return carry

        lax.fori_loop(0, steps, block, 0)

    first = {}

    def take_halo(odd):
        for n in range(steps):
            k = 2 * n + odd
            rows = pl.ds(k * cz, cz)

            @pl.when(me > 0)
            def _():
                remote(dn_s.at[rows], up_r.at[rows], sh.at[k, 1], rh.at[k, 1], (grp, me - 1)).wait_recv()
                own[rows, 0:lead, :] = own[rows, 0:lead, :] + halo_of(up_r[rows])

            @pl.when(me < blocks - 1)
            def _():
                remote(up_s.at[rows], dn_r.at[rows], sh.at[k, 0], rh.at[k, 0], (grp, me + 1)).wait_recv()
                own[rows, py - lead : py, :] = own[rows, py - lead : py, :] + halo_of(dn_r[rows])

            value = jnp.log(own[rows])
            own[rows] = value
            logs_s[rows] = log_code(value)
            for q in range(1, groups):
                peer = lax.rem(grp + q, groups)
                first[k, q] = remote(
                    logs_s.at[k * cz + peer], logs_r.at[k, q - 1], s1.at[k, q - 1], r1.at[k, q - 1], (peer, me)
                )
                first[k, q].start()

    def mean_out(k):
        return remote(mean_s.at[k], lout.at[grp, strip(me)], s2.at[k], r2.at[me], (grp, k))

    def take_logs(odd):
        for n in range(steps):
            k = 2 * n + odd
            total = own[k * cz + grp]
            for q in range(1, groups):
                first[k, q].wait_recv()
                total = total + log_of(logs_r[k, q - 1])
            mean_s[k] = halo_code(jnp.exp(total * (1.0 / groups)))

            @pl.when(me != k)
            def _():
                mean_out(k).start()

            @pl.when(me == k)
            def _():
                lout[grp, strip(me), :] = mean_s[k]

    def pass_on(src, q):
        here = lout.at[grp, strip(src)]
        return remote(here, here, s3.at[src, q - 1], r3.at[src, q - 1], (lax.rem(grp + q, groups), me))

    def take_mean(odd):
        @pl.when(lax.rem(me, 2) == odd)
        def _():
            for rel in range(blocks):
                src = source(rel)
                here = lout.at[grp, strip(src)]
                if rel > 0:
                    remote(here, here, s2.at[src], r2.at[src], (grp, src)).wait_recv()
                for q in range(1, groups):
                    pass_on(src, q).start()

    late(0)
    back(0)
    late(1)
    take_halo(0)
    back(1)
    take_logs(0)
    take_halo(1)
    take_mean(0)
    take_logs(1)
    take_mean(1)

    for k in range(blocks):
        @pl.when(me > 0)
        def _():
            halo(k, True).wait_send()

        @pl.when(me < blocks - 1)
        def _():
            halo(k, False).wait_send()

        @pl.when(me != k)
        def _():
            mean_out(k).wait_send()

        for q in range(1, groups):
            pass_on(k, q).wait_send()
            first[k, q].wait_send()
    @pl.when(jnp.logical_not(double))
    def _():
        for part in range(parts):
            for rel in range(1, blocks):
                for e in range(2):
                    lend(part, source(rel), e).wait_send()

    for copy in sends:
        copy.wait_send()
    for rel in range(blocks):
        src = source(rel)
        for q in range(1, groups):
            peer = lax.rem(grp + groups - q, groups)
            theirs = lout.at[peer, strip(src)]
            remote(theirs, theirs, s3.at[src, q - 1], r3.at[src, q - 1], (peer, me)).wait_recv()


def fused(estimate, measured, tile_plane, tile_strip, view_group, kernel_cols, kernel_rows, kernel_planes):
    cz, ny, nx = estimate.shape
    blocks = lax.axis_size("blk")
    groups = lax.axis_size("grp")
    nz = cz * blocks
    py = ny // blocks
    ranks, width = kernel_rows.shape[1:]
    lead = -(-(width // 2) // 16) * 16
    ext = py + 2 * lead
    per = measured.shape[1] // blocks
    terms = VSLOT * ranks
    bands8 = py // 8
    parts = py // 16
    wide = 8 * nz
    vmem = pl.BlockSpec(memory_space=pltpu.VMEM)
    smem = pl.BlockSpec(memory_space=pltpu.SMEM)
    anym = pl.BlockSpec(memory_space=pl.ANY)
    dma = pltpu.SemaphoreType.DMA
    f32, b16, i16, i32 = jnp.float32, jnp.bfloat16, jnp.int16, jnp.int32
    square = pltpu.VMEM((terms, nx, nx), b16)
    cube = pltpu.VMEM((terms, wide, wide), b16)
    field = pltpu.VMEM((terms * bands8, wide, nx), b16)
    ratio = pltpu.VMEM((VSLOT * 2, wide, nx), b16)
    edge = pltpu.VMEM((nz, lead, nx), i16)
    batch = pltpu.VMEM((parts, blocks, VSLOT * per, 16, nx), b16)
    listing = pltpu.VMEM((blocks, VSLOT * per, 128), i32)
    lout = pl.pallas_call(
        lambda *refs: fused_kernel(blocks, groups, lead, *refs),
        out_shape=jax.ShapeDtypeStruct((cz, ny, nx), i16),
        in_specs=[smem, smem, smem, anym, anym, vmem, vmem, vmem],
        out_specs=vmem,
        scratch_shapes=[
            pltpu.VMEM(estimate.shape, f32),
            pltpu.VMEM(measured.shape, b16),
            pltpu.VMEM((cz, ny + 2 * lead, nx), i16),
            pltpu.VMEM((nz, ext, nx), i16),
            listing,
            batch, batch,
            listing,
            pltpu.VMEM((8, 2 * nx), f32),
            square, square, square, square,
            cube, cube, cube, cube,
            pltpu.VMEM((terms * py, 3 * ext), b16),
            pltpu.VMEM((2 * ext, terms * py), b16),
            pltpu.VMEM((256, 128), f32),
            pltpu.VMEM((wide, 128), i32),
            field, field, field, field,
            ratio, ratio,
            pltpu.VMEM((VSLOT * bands8, wide, nx), f32),
            pltpu.VMEM((VSLOT * bands8, wide, nx), f32),
            pltpu.VMEM((terms * bands8, wide, nx), f32),
            pltpu.VMEM((nz, py, nx), f32),
            edge, edge, edge, edge,
            pltpu.VMEM((nz, py, nx), i16),
            pltpu.VMEM((blocks, groups - 1, py, nx), i16),
            pltpu.VMEM((blocks, py, nx), i16),
            dma((2,)),
            dma((blocks,)), dma((blocks,)),
            dma((blocks, groups - 1)), dma((blocks, groups - 1)),
            dma((blocks,)), dma((blocks,)),
            dma((parts, blocks)), dma((parts, blocks)),
            dma((parts, blocks, 2)), dma((parts, blocks, 2)),
            dma((blocks, 2)), dma((blocks, 2)),
            dma((blocks, groups - 1)), dma((blocks, groups - 1)),
            dma((blocks,)), dma((blocks,)),
            dma((blocks, groups - 1)), dma((blocks, groups - 1)),
        ],
        compiler_params=pltpu.CompilerParams(collective_id=2, has_side_effects=True, vmem_limit_bytes=60 * 2**20),
        name="fused",
    )(view_group, tile_plane, tile_strip, estimate, measured, kernel_cols, kernel_rows, kernel_planes)
    return estimate * halo_of(lout)


def shards(estimate, measured, tile_plane, tile_strip, view_group, kernel_cols, kernel_rows, kernel_planes):
    cz, ny, nx = estimate.shape
    blocks = lax.axis_size("blk")
    groups = lax.axis_size("grp")
    py = ny // blocks
    half = kernel_rows.shape[-1] // 2
    lead = -(-half // 16) * 16
    per = measured.shape[1] // blocks
    fits = (
        cz == groups
        and cz % 2 == 0
        and blocks % 2 == 0
        and py % 16 == 0
        and py >= lead
        and py + 2 * lead <= 128
        and measured.shape[2] == py
        and nx % 128 == 0
        and VSLOT * per == 8
        and groups == 4
        and view_group.shape[0] == groups + 2
        and VSLOT * kernel_rows.shape[1] * py <= 256
        and per * (measured.shape[1] - 1).bit_length() <= 31
        and (8 * cz * blocks) % 128 == 0
        and cz * blocks <= 64
    )
    program = fused if fits else general
    return program(estimate, measured, tile_plane, tile_strip, view_group, kernel_cols, kernel_rows, kernel_planes)


def solution(mesh):
    in_specs = (
        P("blk", None, None),
        P(None, "blk", None, None),
        P(None, "blk"),
        P(None, "blk"),
        P(),
        P(),
        P(),
        P(),
    )
    return jax.shard_map(
        shards, mesh=mesh, in_specs=in_specs, out_specs=P("blk", None, None), check_vma=False
    )
```
